32 devices in a mesh: pa: 8 (over y, x, core), pb: 4 (over z).
Axes of the slice: x: 2, y: 2, z: 4, core: 2. Of those that a mesh axis runs over, the one named last changes fastest.
Arguments:
- queries: bfloat16 [4096, 1024], P(('pa', 'pb')), may hold values from -900 to 900
- batch_hidden: bfloat16 [512, 1024], P(('pa', 'pb')), may hold values from -6 to 6
- pool_hidden: bfloat16 [16384, 1024], P(('pa', 'pb')), may hold values from -6 to 6
- projection: bfloat16 [1024, 1024], replicated, may hold values from -0.1875 to 0.1875
- hard_ids: int32 [4096, 16], P(('pa', 'pb')), may hold values from 0 to 2047, as said below
- query_group: int32 [4096], P(('pa', 'pb')), may hold values from 0 to 63
- labels: int32 [4096], P(('pa', 'pb')), may hold values from 0 to 63
- group_lists: int32 [64, 64], replicated, may hold values from 0 to 127, as said below
Outputs:
- query_grad: bfloat16 [4096, 1024], P(('pa', 'pb'))
- batch_hidden_grad: bfloat16 [512, 1024], P(('pa', 'pb'))
- pool_hidden_grad: bfloat16 [16384, 1024], P(('pa', 'pb'))
The draws below stay inside these ranges and needn't reach their ends.
Inputs may be any that keep to these rules, and one draw needn't show every extreme that they name: `hard_ids`: entry k of a query's list lies in [(k % 4) * 512, (k % 4 + 1) * 512); entries may repeat. `group_lists`: each row holds 64 different values.
All inputs are finite; a program needn't handle non-finite values.
Results may differ from the reference program's by a relative error of at most 0.017.
The reference program's roundings to bfloat16 on the way count: a program that leaves them out, or rounds other values in their place, can miss the bound.
Values may be sent and summed in bfloat16 or wider, within the bound.
No kernel may reach another device: no remote copies, remote signals or barrier semaphores. Data moves between devices by JAX's collectives and lax.ppermute only.
A program may use at most 128 MiB of HBM per device.

```python
import math
import jax
import jax.numpy as jnp
from jax import lax

D = 1024
QD = 128
PD = 512
IB = 16
NGROUPS = 64
HN = 16
GROUP = 64
NQ = 4096
NB = 512
NPOOL = 16384
N_PA = 8
N_PB = 4
DEVICES = 32


def draw_queries(key, part):
    key_one = jax.random.fold_in(jax.random.fold_in(key, 5), 0)
    values_raw = jnp.clip(jax.random.normal(key_one, (NQ, D), jnp.float32), -6.0, 6.0)
    return values_raw.astype(jnp.bfloat16)


def draw_hard_ids(key, part):
    key_one, key_two, key_three = jax.random.split(jax.random.fold_in(key, 11), 3)
    first = jax.random.randint(key_one, (NQ, HN), 0, PD)
    second = jax.random.randint(key_two, (NQ, HN), 0, PD)
    skewed = first * second // max(PD - 1, 1)
    shuffle = jax.random.permutation(key_three, PD)
    owner_index = jnp.arange(HN) % N_PB
    return (owner_index[None, :] * PD + jnp.take(shuffle, skewed)).astype(jnp.int32)


def draw_group_lists(key, part):
    key_list = jax.random.split(jax.random.fold_in(key, 23), NGROUPS)
    rows_all = jax.vmap(lambda one_key: jax.random.permutation(one_key, N_PA * IB)[:GROUP])(key_list)
    return rows_all.astype(jnp.int32)


def plant(entries, own_key, smallest, high):
    longest = entries.shape.index(max(entries.shape))
    spots = []
    for shift in (0, 1):
        where = [jax.random.randint(jax.random.fold_in(own_key, axis), (), 0, length) for axis, length in enumerate(entries.shape)]
        where[longest] = (where[longest] + shift) % entries.shape[longest]
        spots.append(tuple(where))
    return entries.at[spots[0]].set(smallest).at[spots[1]].set(high)


def block_scale(rng, shape, cuts, smallest, high):
    def one(dim, shards_of):
        heights = jax.random.uniform(jax.random.fold_in(jax.random.fold_in(rng, 6), dim), (shards_of,), jnp.float32, smallest / len(cuts), high / len(cuts))
        return jnp.repeat(jnp.exp(heights), shape[dim] // shards_of).reshape((-1,) + (1,) * (len(shape) - dim - 1))

    gain = one(*cuts[0])
    for cut in cuts[1:]:
        gain = gain * one(*cut)
    return gain


def bell_draw(stream_key, shape, spread, limit, cuts=(), kind=jnp.bfloat16):
    loudness = block_scale(stream_key, shape, cuts, -0.22, 0.18) if cuts else 1.0
    array = jax.random.normal(stream_key, shape, jnp.float32) * spread * loudness
    return jnp.minimum(jnp.maximum(array, -limit), limit).astype(kind)


def setup_inputs(seed: int = 0) -> dict:
    keys = jax.random.split(jax.random.key(seed), 9)
    queries = draw_queries(jax.random.fold_in(keys[8], 71), 0)
    batch_hidden = bell_draw(keys[1], (NB, D), 1.0, 6.0, ((0, 32),))
    pool_hidden = bell_draw(keys[2], (NPOOL, D), 1.0, 6.0, ((0, 32),))
    projection = bell_draw(keys[3], (D, D), D ** -0.5, 0.1875)
    hard_ids = draw_hard_ids(jax.random.fold_in(keys[8], 71), 0)
    query_group = plant(jax.random.randint(keys[5], (NQ,), 0, NGROUPS), jax.random.fold_in(keys[5], 1), 0, NGROUPS - 1).astype(jnp.int32)
    labels = plant(jax.random.randint(keys[6], (NQ,), 0, GROUP), jax.random.fold_in(keys[6], 1), 0, GROUP - 1).astype(jnp.int32)
    group_lists = draw_group_lists(jax.random.fold_in(keys[8], 71), 0)
    return {"queries": queries, "batch_hidden": batch_hidden, "pool_hidden": pool_hidden, "projection": projection, "hard_ids": hard_ids, "query_group": query_group, "labels": labels, "group_lists": group_lists}


def reference(queries, batch_hidden, pool_hidden, projection, hard_ids, query_group, labels, group_lists):
    score_scale = 1.0 / math.sqrt(D)
    batch_proj = jnp.dot(batch_hidden, projection, preferred_element_type=jnp.float32).astype(jnp.bfloat16)
    pool_proj = jnp.dot(pool_hidden, projection, preferred_element_type=jnp.float32).astype(jnp.bfloat16)
    batch_table = batch_proj.reshape(N_PA, N_PB, IB, D)
    pool_table = pool_proj.reshape(N_PA, N_PB * PD, D)
    query_blocks = queries.reshape(DEVICES, QD, D)
    hard_blocks = hard_ids.reshape(DEVICES, QD, HN)
    group_blocks = query_group.reshape(DEVICES, QD)
    label_blocks = labels.reshape(DEVICES, QD)
    positions = jnp.arange(GROUP + HN, dtype=jnp.int32)
    query_index = jnp.arange(QD, dtype=jnp.int32)

    def one_block(carry, inputs):
        batch_grad, pool_grad = carry
        device_index, query_block, hard_block, group_block, label_block = inputs
        row_index = (device_index // N_PB).astype(jnp.int32)
        col_index = (device_index % N_PB).astype(jnp.int32)
        column = lax.dynamic_index_in_dim(batch_table, col_index, 1, keepdims=False).reshape(N_PA * IB, D)
        pool_row = lax.dynamic_index_in_dim(pool_table, row_index, 0, keepdims=False)
        chosen = jnp.take(group_lists, group_block, axis=0)
        group_rows = jnp.take(column, chosen, axis=0).astype(jnp.float32)
        hard_rows = jnp.take(pool_row, hard_block, axis=0).astype(jnp.float32)
        query_wide = query_block.astype(jnp.float32)
        group_scores = score_scale * jnp.einsum('id,icd->ic', query_wide, group_rows, precision=lax.Precision.HIGHEST)
        hard_scores = score_scale * jnp.einsum('id,ikd->ik', query_wide, hard_rows, precision=lax.Precision.HIGHEST)
        scores = jnp.concatenate([group_scores, hard_scores], axis=1)
        likely = jax.nn.softmax(scores, axis=1)
        target = (positions[None, :] == label_block[:, None]).astype(jnp.float32)
        dscore = lax.optimization_barrier((likely - target).astype(jnp.bfloat16)).astype(jnp.float32)
        grad_group = dscore[:, :GROUP]
        grad_hard = dscore[:, GROUP:]
        query_grad = score_scale * (jnp.einsum('ic,icd->id', grad_group, group_rows, precision=lax.Precision.HIGHEST) + jnp.einsum('ik,ikd->id', grad_hard, hard_rows, precision=lax.Precision.HIGHEST))
        dense_grad = jnp.zeros((QD, N_PA * IB), jnp.float32).at[query_index[:, None], chosen].add(grad_group)
        batch_part = score_scale * jnp.dot(dense_grad.T, query_wide, precision=lax.Precision.HIGHEST)
        batch_part = batch_part.reshape(N_PA, 1, IB, D)
        zero_index = jnp.zeros((), jnp.int32)
        start = (zero_index, col_index, zero_index, zero_index)
        current = lax.dynamic_slice(batch_grad, start, (N_PA, 1, IB, D))
        batch_grad = lax.dynamic_update_slice(batch_grad, current + batch_part, start)
        contrib = score_scale * grad_hard[:, :, None] * query_wide[:, None, :]
        contrib = lax.optimization_barrier(contrib.astype(jnp.bfloat16)).astype(jnp.float32)
        global_rows = (row_index * (N_PB * PD) + hard_block).astype(jnp.int32)
        pool_grad = pool_grad.at[global_rows.reshape(-1)].add(contrib.reshape(QD * HN, D))
        return ((batch_grad, pool_grad), query_grad.astype(jnp.bfloat16))
    start_carry = (jnp.zeros((N_PA, N_PB, IB, D), jnp.float32), jnp.zeros((NPOOL, D), jnp.float32))
    device_list = jnp.arange(DEVICES, dtype=jnp.int32)
    (batch_grad, pool_grad), grads = lax.scan(one_block, start_carry, (device_list, query_blocks, hard_blocks, group_blocks, label_blocks))
    dims = (((1,), (1,)), ((), ()))
    batch_low = batch_grad.reshape(NB, D).astype(jnp.bfloat16)
    pool_low = pool_grad.astype(jnp.bfloat16)
    batch_hidden_grad = lax.dot_general(batch_low, projection, dims, preferred_element_type=jnp.float32).astype(jnp.bfloat16)
    pool_hidden_grad = lax.dot_general(pool_low, projection, dims, preferred_element_type=jnp.float32).astype(jnp.bfloat16)
    return (grads.reshape(NQ, D), batch_hidden_grad, pool_hidden_grad)
```

```python
import functools
import math

import jax
import jax.numpy as jnp
from jax import lax
from jax.experimental import pallas as pl
from jax.experimental.pallas import tpu as pltpu
from jax.sharding import PartitionSpec as P

F32 = jnp.float32
BF16 = jnp.bfloat16
LANE_BASE = 16


def nt(a, b):
    return lax.dot_general(a, b, (((1,), (1,)), ((), ())), preferred_element_type=F32)


def tn(a, b):
    return lax.dot_general(a, b, (((0,), (0,)), ((), ())), preferred_element_type=F32)


def local_ids(packed_ref, me, rows, owners, per):
    width = rows
    found = None
    for owner in range(owners):
        parts = []
        for j in range(per):
            k = owner * per + j
            block, sub = divmod(k, 8)
            high = packed_ref[rows : rows + 8, 2 * block * width : (2 * block + 1) * width]
            low = packed_ref[rows : rows + 8, (2 * block + 1) * width : (2 * block + 2) * width]
            ids = high.astype(F32) * LANE_BASE + low.astype(F32)
            parts.append(ids[sub : sub + 1, :])
        if found is None:
            found = parts
        else:
            found = [jnp.where(me == owner, new, old) for new, old in zip(parts, found)]
    return found


def owner_kernel(rows, owners, per, scale, me_ref, packed_ref, table_ref, score_ref, term_ref):
    me = me_ref[0]
    count = table_ref.shape[0]
    ids = local_ids(packed_ref, me, rows, owners, per)
    query = packed_ref[:rows, :]
    dense = nt(table_ref[...], query)
    row_iota = lax.broadcasted_iota(jnp.int32, (count, rows), 0).astype(F32)
    hits = [row_iota == one for one in ids]
    scores = [jnp.sum(jnp.where(hit, dense, 0.0), axis=0, keepdims=True) * scale for hit in hits]
    top = functools.reduce(jnp.maximum, scores)
    weight = jnp.zeros((count, rows), F32)
    for hit, one in zip(hits, scores):
        weight = weight + jnp.where(hit, jnp.exp(one - top), 0.0)
    for j, one in enumerate(scores):
        score_ref[j : j + 1, :] = one
    term_ref[...] = tn(weight.astype(BF16), table_ref[...]).astype(BF16)


def group_kernel(scale, query_ref, column_ref, group_ref, lists_ref, score_ref, place_ref):
    rows = query_ref.shape[0]
    groups, size = lists_ref.shape
    count = column_ref.shape[0]
    score_ref[...] = nt(column_ref[...], query_ref[...]) * scale
    column_iota = lax.broadcasted_iota(jnp.int32, (groups, count), 1)
    places = jnp.zeros((groups, count), F32)
    lists = lists_ref[...]
    for c in range(size):
        places = places + jnp.where(lists[:, c : c + 1] == column_iota, float(c + 1), 0.0)
    group_iota = lax.broadcasted_iota(jnp.int32, (groups, rows), 0)
    mine = (group_iota == group_ref[...]).astype(BF16)
    place_ref[...] = tn(places.astype(BF16), mine)


def soft_kernel(owners, per, scale, *refs):
    score_ref, place_ref, label_ref, query_ref, column_ref, own_term_ref = refs[:6]
    hard_refs = refs[6 : 6 + owners]
    grad_refs = refs[6 + owners : 6 + 2 * owners]
    part_ref, sum_ref, factor_ref = refs[6 + 2 * owners :]
    rows = query_ref.shape[0]
    place = place_ref[...]
    member = place > 0.5
    dense = score_ref[...]
    tops = [jnp.max(ref[...], axis=0, keepdims=True) for ref in hard_refs]
    top = jnp.max(jnp.where(member, dense, -jnp.inf), axis=0, keepdims=True)
    top = functools.reduce(jnp.maximum, tops, top)
    power = jnp.where(member, jnp.exp(jnp.where(member, dense - top, 0.0)), 0.0)
    hard = [jnp.exp(ref[...] - top) for ref in hard_refs]
    total = jnp.sum(power, axis=0, keepdims=True)
    for one in hard:
        total = total + jnp.sum(one, axis=0, keepdims=True)
    target = (place == (label_ref[...] + 1).astype(F32)).astype(F32)
    grad = jnp.where(member, power / total - target, 0.0).astype(BF16)
    for ref, one in zip(grad_refs, hard):
        ref[...] = (one / total).astype(BF16)
    part_ref[...] = (
        lax.dot_general(grad, query_ref[...], (((1,), (0,)), ((), ())), preferred_element_type=F32)
        * scale
    ).astype(BF16)
    factor = [jnp.exp(one - top) / total for one in tops]
    factor = jnp.concatenate(factor + [jnp.zeros((rows - owners, rows), F32)], axis=0)
    factor = factor.T
    factor_ref[...] = factor
    sum_ref[...] = tn(grad, column_ref[...]) + factor[:, :1] * own_term_ref[...].astype(F32)


def pool_kernel(rows, owners, per, scale, me_ref, *refs):
    packed_refs = refs[:owners]
    grad_refs = refs[owners : 2 * owners]
    out_ref = refs[2 * owners]
    me = me_ref[0]
    count = out_ref.shape[0]
    row_iota = lax.broadcasted_iota(jnp.int32, (count, rows), 0).astype(F32)
    total = None
    for packed_ref, grad_ref in zip(packed_refs, grad_refs):
        ids = local_ids(packed_ref, me, rows, owners, per)
        grad = grad_ref[...].astype(F32)
        weight = jnp.zeros((count, rows), F32)
        for j, one in enumerate(ids):
            weight = weight + jnp.where(row_iota == one, grad[j : j + 1, :], 0.0)
        part = jnp.dot(
            weight.astype(BF16), packed_ref[:rows, :], preferred_element_type=F32
        )
        total = part if total is None else total + part
    out_ref[...] = (total * scale).astype(BF16)


def whole(count):
    return [pl.BlockSpec(memory_space=pltpu.VMEM)] * count


def call(kernel, outs, arrays, scalars=(), flops=0):
    outs = [jax.ShapeDtypeStruct(*one) for one in outs]
    moved = sum(a.size * a.dtype.itemsize for a in list(arrays) + outs)
    return pl.pallas_call(
        kernel,
        out_shape=outs,
        in_specs=[pl.BlockSpec(memory_space=pltpu.SMEM)] * len(scalars) + whole(len(arrays)),
        out_specs=whole(len(outs)),
        cost_estimate=pl.CostEstimate(flops=flops, bytes_accessed=moved, transcendentals=0),
    )(*scalars, *arrays)


def shards(
    queries, batch_hidden, pool_hidden, projection, hard_ids, query_group, labels, group_lists
):
    rows, depth = queries.shape
    scale = 1.0 / math.sqrt(depth)
    owners = lax.axis_size("pb")
    pool_count = pool_hidden.shape[0]
    hard_count = hard_ids.shape[1]
    per = hard_count // owners
    me = lax.axis_index("pb").astype(jnp.int32).reshape(1)

    ids = hard_ids.T.reshape(per, owners, rows).transpose(1, 0, 2)
    ids = ids - (jnp.arange(owners, dtype=jnp.int32) * pool_count)[:, None, None]
    ids = ids.reshape(hard_count // 8, 8, rows)
    pieces = []
    for block in range(hard_count // 8):
        pieces.append((ids[block] // LANE_BASE).astype(BF16))
        pieces.append((ids[block] % LANE_BASE).astype(BF16))
    tail = jnp.concatenate(pieces, axis=1)
    tail = jnp.pad(tail, ((0, 0), (0, depth - tail.shape[1])))
    packed = jnp.concatenate([queries, tail], axis=0)

    def shift(x, k):
        return lax.ppermute(x, "pb", [(i, (i + k) % owners) for i in range(owners)])

    blocks = [packed] + [shift(packed, k) for k in range(1, owners)]
    hidden = lax.all_gather(batch_hidden, "pa", axis=0, tiled=True)
    table = jnp.dot(pool_hidden, projection, preferred_element_type=F32).astype(BF16)
    column = jnp.dot(hidden, projection, preferred_element_type=F32).astype(BF16)
    column_count = column.shape[0]

    scores, place = call(
        functools.partial(group_kernel, scale),
        [((column_count, rows), F32), ((column_count, rows), F32)],
        [queries, column, query_group[None, :], group_lists],
        flops=2 * rows * column_count * depth,
    )
    hards, terms = [], []
    for block in blocks:
        hard, term = call(
            functools.partial(owner_kernel, rows, owners, per, scale),
            [((per, rows), F32), ((rows, depth), BF16)],
            [block, table],
            [me],
            flops=4 * rows * pool_count * depth,
        )
        hards.append(hard)
        terms.append(term)
    hards = [hards[0]] + [shift(hards[k], owners - k) for k in range(1, owners)]
    terms = [terms[0]] + [shift(terms[k], owners - k) for k in range(1, owners)]
    outs = call(
        functools.partial(soft_kernel, owners, per, scale),
        [((per, rows), BF16)] * owners
        + [((column_count, depth), BF16), ((rows, depth), F32), ((rows, rows), F32)],
        [scores, place, labels[None, :], queries, column, terms[0]] + hards,
        flops=4 * rows * column_count * depth,
    )
    grads, (part, total, factor) = outs[:owners], outs[owners:]
    grads = [grads[0]] + [shift(grads[k], k) for k in range(1, owners)]
    part = part.reshape(-1, batch_hidden.shape[0], depth)
    part = lax.all_to_all(part, "pa", split_axis=0, concat_axis=0, tiled=True)
    batch_grad = jnp.sum(part.astype(F32), axis=0).astype(BF16)
    batch_hidden_grad = nt(batch_grad, projection).astype(BF16)
    (pool_grad,) = call(
        functools.partial(pool_kernel, rows, owners, per, scale),
        [((pool_count, depth), BF16)],
        blocks + grads,
        [me],
        flops=2 * rows * owners * pool_count * depth,
    )
    pool_hidden_grad = nt(pool_grad, projection).astype(BF16)
    for k in range(1, owners):
        total = total + factor[:, k : k + 1] * terms[k].astype(F32)
    query_grad = (scale * total).astype(BF16)
    return (query_grad, batch_hidden_grad, pool_hidden_grad)


def solution(mesh):
    return jax.shard_map(
        shards,
        mesh=mesh,
        in_specs=(
            P(("pa", "pb"), None),
            P(("pa", "pb"), None),
            P(("pa", "pb"), None),
            P(),
            P(("pa", "pb"), None),
            P(("pa", "pb")),
            P(("pa", "pb")),
            P(),
        ),
        out_specs=(P(("pa", "pb"), None), P(("pa", "pb"), None), P(("pa", "pb"), None)),
        check_vma=False,
    )
```

```python
import functools
import math

import jax
import jax.numpy as jnp
from jax import lax
from jax.experimental import pallas as pl
from jax.experimental.pallas import tpu as pltpu
from jax.sharding import PartitionSpec as P

F32 = jnp.float32
BF16 = jnp.bfloat16
LOW_BITS = 4
SUB = 8
VMEM_LIMIT = 8 << 20


def nn(a, b):
    return lax.dot_general(a, b, (((1,), (0,)), ((), ())), preferred_element_type=F32)


def nt(a, b):
    return lax.dot_general(a, b, (((1,), (1,)), ((), ())), preferred_element_type=F32)


def tn(a, b):
    return lax.dot_general(a, b, (((0,), (0,)), ((), ())), preferred_element_type=F32)


def pack_kernel(owners, pool_count, ids_ref, query_ref, packed_ref, sem):
    rows, depth = query_ref.shape
    hard_count = ids_ref.shape[0]
    per = hard_count // owners
    copy = pltpu.make_async_copy(query_ref, packed_ref.at[:rows, :], sem)
    copy.start()
    packed_ref[rows:, :] = jnp.zeros((SUB, depth), BF16)
    for block in range(hard_count // SUB):
        lines = []
        for place in range(block * SUB, (block + 1) * SUB):
            owner, j = divmod(place, per)
            k = j * owners + owner
            lines.append(ids_ref[k : k + 1, :] - owner * pool_count)
        ids = jnp.concatenate(lines, axis=0)
        high = jnp.right_shift(ids, LOW_BITS)
        low = ids - jnp.left_shift(high, LOW_BITS)
        start = 2 * block * rows
        packed_ref[rows:, start : start + rows] = high.astype(F32).astype(BF16)
        packed_ref[rows:, start + rows : start + 2 * rows] = low.astype(F32).astype(BF16)
    copy.wait()


def local_ids(packed_ref, me, rows, owners, per):
    found = None
    for owner in range(owners):
        parts = []
        for j in range(per):
            block, sub = divmod(owner * per + j, SUB)
            start = 2 * block * rows
            high = packed_ref[rows:, start : start + rows].astype(F32)
            low = packed_ref[rows:, start + rows : start + 2 * rows].astype(F32)
            ids = high * float(1 << LOW_BITS) + low
            parts.append(ids[sub : sub + 1, :])
        if found is None:
            found = parts
        else:
            found = [jnp.where(me == owner, new, old) for new, old in zip(parts, found)]
    return found


def score_block(me, packed_ref, table_ref, rows, owners, per, scale):
    count = table_ref.shape[0]
    ids = local_ids(packed_ref, me, rows, owners, per)
    dense = nt(table_ref[...], packed_ref[:rows, :])
    row_iota = lax.broadcasted_iota(jnp.int32, (count, rows), 0).astype(F32)
    hits = [row_iota == one for one in ids]
    scores = [jnp.sum(jnp.where(hit, dense, 0.0), axis=0, keepdims=True) * scale for hit in hits]
    top = functools.reduce(jnp.maximum, scores)
    powers = [jnp.exp(one - top) for one in scores]
    weight = jnp.zeros((count, rows), F32)
    for hit, one in zip(hits, powers):
        weight = weight + jnp.where(hit, one, 0.0)
    return weight, top, functools.reduce(jnp.add, powers)


def own_kernel(owners, per, scale, packed_ref, hidden_ref, projection_ref, *outs):
    table_ref, turned_ref, stat_ref, weight_ref, term_ref = outs
    me = lax.axis_index("pb")
    rows = packed_ref.shape[0] - SUB
    table_ref[...] = nn(hidden_ref[...], projection_ref[...]).astype(BF16)
    turned_ref[...] = nt(packed_ref[:rows, :], projection_ref[...]).astype(BF16)
    weight, top, total = score_block(me, packed_ref, table_ref, rows, owners, per, scale)
    stat_ref[0:1, :] = top
    stat_ref[1:2, :] = total
    weight_ref[...] = weight
    term_ref[...] = tn(weight.astype(BF16), table_ref[...]).astype(BF16)


def far_kernel(owners, per, scale, table_ref, own_stat_ref, group_stat_ref, *refs):
    far = owners - 1
    me = lax.axis_index("pb")
    packed_refs, stat_ref = refs[:far], refs[far]
    weight_refs, term_refs = refs[owners : owners + far], refs[owners + far :]
    rows = packed_refs[0].shape[0] - SUB
    stat_ref[0:2, :] = own_stat_ref[...]
    stat_ref[2 * owners :, :] = group_stat_ref[...]
    for slot in range(1, owners):
        packed_ref = packed_refs[slot - 1]
        weight, top, total = score_block(me, packed_ref, table_ref, rows, owners, per, scale)
        stat_ref[2 * slot : 2 * slot + 1, :] = top
        stat_ref[2 * slot + 1 : 2 * slot + 2, :] = total
        weight_refs[slot - 1][...] = weight
        term_refs[slot - 1][...] = tn(weight.astype(BF16), table_ref[...]).astype(BF16)


def turn_kernel(count, projection_ref, *refs):
    for packed_ref, out_ref in zip(refs[:count], refs[-count:]):
        rows = out_ref.shape[0]
        out_ref[...] = nt(packed_ref[:rows, :], projection_ref[...]).astype(BF16)


def group_kernel(scale, query_ref, hidden_ref, projection_ref, group_ref, lists_ref, *outs):
    column_ref, power_ref, place_ref, stat_ref = outs
    rows = query_ref.shape[0]
    groups, size = lists_ref.shape
    count = column_ref.shape[0]
    column_ref[...] = nn(hidden_ref[...], projection_ref[...]).astype(BF16)
    dense = nt(column_ref[...], query_ref[...]) * scale
    column_iota = lax.broadcasted_iota(jnp.int32, (groups, count), 1)
    places = jnp.zeros((groups, count), F32)
    lists = lists_ref[...]
    for c in range(size):
        places = places + jnp.where(lists[:, c : c + 1] == column_iota, float(c + 1), 0.0)
    group_iota = lax.broadcasted_iota(jnp.int32, (groups, rows), 0)
    mine = (group_iota == group_ref[...]).astype(F32).astype(BF16)
    place = tn(places.astype(BF16), mine)
    member = place > 0.5
    top = jnp.max(jnp.where(member, dense, -jnp.inf), axis=0, keepdims=True)
    power = jnp.where(member, jnp.exp(jnp.where(member, dense - top, 0.0)), 0.0)
    power_ref[...] = power
    place_ref[...] = place
    stat_ref[0:1, :] = top
    stat_ref[1:2, :] = jnp.sum(power, axis=0, keepdims=True)


def totals(stat_refs, owners, source):
    group_ref = stat_refs[source]
    tops = [group_ref[2 * owners : 2 * owners + 1, :]]
    sums = [group_ref[2 * owners + 1 : 2 * owners + 2, :]]
    for step, ref in enumerate(stat_refs):
        slot = (source - step) % owners
        tops.append(ref[2 * slot : 2 * slot + 1, :])
        sums.append(ref[2 * slot + 1 : 2 * slot + 2, :])
    top = functools.reduce(jnp.maximum, tops)
    total = functools.reduce(jnp.add, [s * jnp.exp(t - top) for s, t in zip(sums, tops)])
    return top, total


def soft_kernel(owners, scale, *refs):
    power_ref, place_ref, label_ref, query_ref, column_ref, own_term_ref = refs[:6]
    stat_refs = refs[6 : 6 + owners]
    keep_ref, give_ref, sum_ref, factor_ref = refs[6 + owners :]
    rows = query_ref.shape[0]
    top, total = totals(stat_refs, owners, 0)
    place = place_ref[...]
    target = (place == (label_ref[...] + 1).astype(F32)).astype(F32)
    group_top = stat_refs[0][2 * owners : 2 * owners + 1, :]
    likely = power_ref[...] * jnp.exp(group_top - top) / total
    grad = jnp.where(place > 0.5, likely - target, 0.0)
    kept, _, size, _ = halves = (keep_ref.shape[0], 2, keep_ref.shape[1], rows)
    even, odd = grad.reshape(halves)[:, 0], grad.reshape(halves)[:, 1]
    first = lax.rem(lax.axis_index("pa"), 2) == 0
    mine = jnp.where(first, even, odd).reshape(kept * size, rows).astype(BF16)
    other = jnp.where(first, odd, even).reshape(kept * size, rows).astype(BF16)
    give_ref[...] = (nn(other, query_ref[...]) * scale).astype(BF16)
    keep_ref[...] = (nn(mine, query_ref[...]) * scale).reshape(keep_ref.shape)
    factor = []
    for slot in range(owners):
        ref = stat_refs[(owners - slot) % owners]
        factor.append(jnp.exp(ref[2 * slot : 2 * slot + 1, :] - top) / total)
    factor = jnp.concatenate(factor + [jnp.zeros((rows - owners, rows), F32)], axis=0).T
    factor_ref[...] = factor
    own = factor[:, :1] * own_term_ref[...].astype(F32)
    sum_ref[...] = tn(grad.astype(BF16), column_ref[...]) + own


def merge_kernel(keep_ref, got_ref, own_ref, *outs):
    pairs = keep_ref.shape[0]
    pair = lax.div(lax.axis_index("pa"), 2)
    own_ref[...] = keep_ref[pair] + got_ref[pair].astype(F32)
    for step in range(1, pairs):
        to = lax.rem(pair + step, pairs)
        outs[step - 1][...] = (keep_ref[to] + got_ref[to].astype(F32)).astype(BF16)


def pool_kernel(owners, scale, *refs):
    stat_refs = refs[:owners]
    weight_refs = refs[owners : 2 * owners]
    turned_refs = refs[2 * owners : 3 * owners]
    out_ref = refs[3 * owners]
    acc = None
    for source in range(owners):
        top, total = totals(stat_refs, owners, source)
        factor = jnp.exp(stat_refs[0][2 * source : 2 * source + 1, :] - top) / total
        part = nn((weight_refs[source][...] * factor).astype(BF16), turned_refs[source][...])
        acc = part if acc is None else acc + part
    out_ref[...] = (acc * scale).astype(BF16)


def batch_kernel(projection_ref, own_ref, *refs):
    total = own_ref[...]
    for ref in refs[:-1]:
        total = total + ref[...].astype(F32)
    refs[-1][...] = nt(total.astype(BF16), projection_ref[...]).astype(BF16)


def query_kernel(owners, scale, sum_ref, factor_ref, *refs):
    out_ref = refs[-1]
    total = sum_ref[...]
    for slot in range(1, owners):
        total = total + factor_ref[:, slot : slot + 1] * refs[slot - 1][...].astype(F32)
    out_ref[...] = (total * scale).astype(BF16)


def call(kernel, outs, arrays, after=(), flops=0, in_place=(), scratch=()):
    outs = [jax.ShapeDtypeStruct(*one) for one in outs]
    arrays = list(arrays) + list(in_place)
    moved = sum(a.size * a.dtype.itemsize for a in arrays + outs)
    count, waits = len(arrays), len(after)
    vmem = pl.BlockSpec(memory_space=pltpu.VMEM)

    def body(*refs):
        kernel(*refs[:count], *refs[count + waits :])

    results = pl.pallas_call(
        body,
        out_shape=outs,
        in_specs=[vmem] * (len(arrays) - len(in_place))
        + [pl.BlockSpec(memory_space=pltpu.HBM)] * len(in_place)
        + [pl.BlockSpec(memory_space=pl.ANY)] * waits,
        out_specs=[vmem] * len(outs),
        scratch_shapes=list(scratch),
        compiler_params=pltpu.CompilerParams(vmem_limit_bytes=VMEM_LIMIT),
        cost_estimate=pl.CostEstimate(flops=flops, bytes_accessed=moved, transcendentals=0),
    )(*arrays, *after)
    return list(results)


def shards(
    queries, batch_hidden, pool_hidden, projection, hard_ids, query_group, labels, group_lists
):
    rows, depth = queries.shape
    scale = 1.0 / math.sqrt(depth)
    owners = lax.axis_size("pb")
    pool_count = pool_hidden.shape[0]
    per = hard_ids.shape[1] // owners
    column_count = batch_hidden.shape[0] * lax.axis_size("pa")
    term, weight = ((rows, depth), BF16), ((pool_count, rows), F32)

    def shift(x, k):
        return lax.ppermute(x, "pb", [(i, (i + k) % owners) for i in range(owners)])

    (packed,) = call(
        functools.partial(pack_kernel, owners, pool_count),
        [((rows + SUB, depth), BF16)],
        [hard_ids.T],
        in_place=[queries],
        scratch=[pltpu.SemaphoreType.DMA],
    )
    far = [shift(packed, k) for k in range(1, owners)]
    hidden = lax.all_gather(batch_hidden, "pa", axis=0, tiled=True)
    table, turned, own_stat, own_weight, own_term = call(
        functools.partial(own_kernel, owners, per, scale),
        [((pool_count, depth), BF16), term, ((2, rows), F32), weight, term],
        [packed, pool_hidden, projection],
        flops=2 * depth * (pool_count * depth + rows * depth + 2 * rows * pool_count),
    )
    column, power, place, group_stat = call(
        functools.partial(group_kernel, scale),
        [
            ((column_count, depth), BF16),
            ((column_count, rows), F32),
            ((column_count, rows), F32),
            ((2, rows), F32),
        ],
        [queries, hidden, projection, query_group[None, :], group_lists],
        flops=2 * depth * column_count * (rows + depth),
    )
    outs = call(
        functools.partial(far_kernel, owners, per, scale),
        [((2 * owners + 2, rows), F32)] + [weight] * (owners - 1) + [term] * (owners - 1),
        [table, own_stat, group_stat] + far,
        flops=4 * (owners - 1) * rows * pool_count * depth,
    )
    stat, weights, terms = outs[0], [own_weight] + outs[1:owners], outs[owners:]
    stats = [stat] + [shift(stat, k) for k in range(1, owners)]
    terms = [shift(terms[k - 1], owners - k) for k in range(1, owners)]
    turned = [turned] + call(
        functools.partial(turn_kernel, owners - 1),
        [term] * (owners - 1),
        [projection] + far,
        after=[stat],
        flops=2 * (owners - 1) * rows * depth * depth,
    )
    members, size = lax.axis_size("pa"), batch_hidden.shape[0]
    pairs = members // 2
    keep, give, total, factor = call(
        functools.partial(soft_kernel, owners, scale),
        [
            ((pairs, size, depth), F32),
            ((pairs * size, depth), BF16),
            ((rows, depth), F32),
            ((rows, rows), F32),
        ],
        [power, place, labels[None, :], queries, column, own_term] + stats,
        after=turned[1:2],
        flops=4 * rows * column_count * depth,
    )
    got = lax.ppermute(give, "pa", [(i, i ^ 1) for i in range(members)])
    parts = call(
        merge_kernel,
        [((size, depth), F32)] + [((size, depth), BF16)] * (pairs - 1),
        [keep, got.reshape(pairs, size, depth)],
        flops=column_count * depth,
    )
    for step in range(1, pairs):
        to = [(i, (i + 2 * step) % members) for i in range(members)]
        parts[step] = lax.ppermute(parts[step], "pa", to)
    (pool_hidden_grad,) = call(
        functools.partial(pool_kernel, owners, scale),
        [((pool_count, depth), BF16)],
        stats + weights + turned,
        flops=2 * rows * owners * pool_count * depth,
    )
    (batch_hidden_grad,) = call(
        batch_kernel,
        [(batch_hidden.shape, BF16)],
        [projection] + parts,
        flops=2 * batch_hidden.shape[0] * depth * depth,
    )
    (query_grad,) = call(
        functools.partial(query_kernel, owners, scale),
        [((rows, depth), BF16)],
        [total, factor] + terms,
        flops=4 * rows * depth * owners,
    )
    return (query_grad, batch_hidden_grad, pool_hidden_grad)


def solution(mesh):
    return jax.shard_map(
        shards,
        mesh=mesh,
        in_specs=(
            P(("pa", "pb"), None),
            P(("pa", "pb"), None),
            P(("pa", "pb"), None),
            P(),
            P(("pa", "pb"), None),
            P(("pa", "pb")),
            P(("pa", "pb")),
            P(),
        ),
        out_specs=(P(("pa", "pb"), None), P(("pa", "pb"), None), P(("pa", "pb"), None)),
        check_vma=False,
    )
```

```python
import functools
import math

import jax
import jax.numpy as jnp
from jax import lax
from jax.experimental import pallas as pl
from jax.experimental.pallas import tpu as pltpu
from jax.sharding import PartitionSpec as P


F32 = jnp.float32
BF16 = jnp.bfloat16
LOW_BITS = 4
SUB = 8
VMEM_LIMIT = 8 << 20


def nn(a, b):
    return lax.dot_general(a, b, (((1,), (0,)), ((), ())), preferred_element_type=F32)


def nt(a, b):
    return lax.dot_general(a, b, (((1,), (1,)), ((), ())), preferred_element_type=F32)


def tn(a, b):
    return lax.dot_general(a, b, (((0,), (0,)), ((), ())), preferred_element_type=F32)


def pack_kernel(owners, pool_count, ids_ref, query_ref, packed_ref, sem):
    rows, depth = query_ref.shape
    hard_count = ids_ref.shape[0]
    per = hard_count // owners
    copy = pltpu.make_async_copy(query_ref, packed_ref.at[:rows, :], sem)
    copy.start()
    packed_ref[rows:, :] = jnp.zeros((SUB, depth), BF16)
    for block in range(hard_count // SUB):
        lines = []
        for place in range(block * SUB, (block + 1) * SUB):
            owner, j = divmod(place, per)
            k = j * owners + owner
            lines.append(ids_ref[k : k + 1, :] - owner * pool_count)
        ids = jnp.concatenate(lines, axis=0)
        high = jnp.right_shift(ids, LOW_BITS)
        low = ids - jnp.left_shift(high, LOW_BITS)
        start = 2 * block * rows
        packed_ref[rows:, start : start + rows] = high.astype(F32).astype(BF16)
        packed_ref[rows:, start + rows : start + 2 * rows] = low.astype(F32).astype(BF16)
    copy.wait()


def local_ids(packed_ref, me, rows, owners, per):
    found = None
    for owner in range(owners):
        parts = []
        for j in range(per):
            block, sub = divmod(owner * per + j, SUB)
            start = 2 * block * rows
            high = packed_ref[rows:, start : start + rows].astype(F32)
            low = packed_ref[rows:, start + rows : start + 2 * rows].astype(F32)
            ids = high * float(1 << LOW_BITS) + low
            parts.append(ids[sub : sub + 1, :])
        if found is None:
            found = parts
        else:
            found = [jnp.where(me == owner, new, old) for new, old in zip(parts, found)]
    return found


def score_block(me, packed_ref, table_ref, rows, owners, per, scale):
    count = table_ref.shape[0]
    ids = local_ids(packed_ref, me, rows, owners, per)
    dense = nt(table_ref[...], packed_ref[:rows, :])
    row_iota = lax.broadcasted_iota(jnp.int32, (count, rows), 0).astype(F32)
    hits = [row_iota == one for one in ids]
    scores = [jnp.sum(jnp.where(hit, dense, 0.0), axis=0, keepdims=True) * scale for hit in hits]
    top = functools.reduce(jnp.maximum, scores)
    powers = [jnp.exp(one - top) for one in scores]
    weight = jnp.zeros((count, rows), F32)
    for hit, one in zip(hits, powers):
        weight = weight + jnp.where(hit, one, 0.0)
    return weight, top, functools.reduce(jnp.add, powers)


def own_kernel(owners, per, scale, packed_ref, hidden_ref, projection_ref, *outs):
    table_ref, turned_ref, stat_ref, weight_ref, term_ref = outs
    me = lax.axis_index("pb")
    rows = packed_ref.shape[0] - SUB
    table_ref[...] = nn(hidden_ref[...], projection_ref[...]).astype(BF16)
    turned_ref[...] = nt(packed_ref[:rows, :], projection_ref[...]).astype(BF16)
    weight, top, total = score_block(me, packed_ref, table_ref, rows, owners, per, scale)
    stat_ref[0:1, :] = top
    stat_ref[1:2, :] = total
    weight_ref[...] = weight
    term_ref[...] = tn(weight.astype(BF16), table_ref[...]).astype(BF16)


def score_kernel(owners, per, scale, table_ref, packed_ref, stat_ref, weight_ref):
    rows = packed_ref.shape[0] - SUB
    me = lax.axis_index("pb")
    weight, top, total = score_block(me, packed_ref, table_ref, rows, owners, per, scale)
    stat_ref[0:1, :] = top
    stat_ref[1:2, :] = total
    weight_ref[...] = weight


def term_kernel(table_ref, stat_ref, weight_ref, *refs):
    old_ref, out_ref = refs if len(refs) == 2 else (None, refs[0])
    weight, top = weight_ref[...], stat_ref[0:1, :]
    rows = weight.shape[1]
    if old_ref is not None:
        parts = [old_ref[rows:, k * rows : (k + 1) * rows].astype(F32)[0:1, :] for k in range(3)]
        before = parts[0] + parts[1] + parts[2]
        both = jnp.maximum(before, top)
        weight = weight * jnp.exp(top - both)
        column = jnp.broadcast_to(jnp.exp(before - both), (rows, rows)).T[:, :1]
        top = both
    term = tn(weight.astype(BF16), table_ref[...])
    if old_ref is not None:
        term = term + column * old_ref[:rows, :].astype(F32)
    out_ref[:rows, :] = term.astype(BF16)
    if out_ref.shape[0] > rows:
        out_ref[rows:, :] = jnp.zeros((SUB, out_ref.shape[1]), BF16)
        left = jnp.broadcast_to(top, (SUB, rows))
        for k in range(3):
            part = left.astype(BF16)
            out_ref[rows:, k * rows : (k + 1) * rows] = part
            left = left - part.astype(F32)


def join_kernel(*refs):
    for k, ref in enumerate(refs[:-1]):
        refs[-1][2 * k : 2 * k + 2, :] = ref[...]


def pair_kernel(mine_ref, other_ref, out_ref):
    first = lax.rem(lax.axis_index("pa"), 2) == 0
    mine, other = mine_ref[...], other_ref[...]
    out_ref[0] = jnp.where(first, mine, other)
    out_ref[1] = jnp.where(first, other, mine)


def turn_kernel(count, projection_ref, *refs):
    for packed_ref, out_ref in zip(refs[:count], refs[-count:]):
        rows = out_ref.shape[0]
        out_ref[...] = nt(packed_ref[:rows, :], projection_ref[...]).astype(BF16)


def group_kernel(scale, pairs, query_ref, projection_ref, group_ref, lists_ref, *refs):
    column_ref, power_ref, place_ref, stat_ref, hidden_ref = refs[pairs:]
    rows = query_ref.shape[0]
    groups, size = lists_ref.shape
    count = column_ref.shape[0]
    pair = lax.div(lax.axis_index("pa"), 2)
    for step, ref in enumerate(refs[:pairs]):
        hidden_ref[lax.rem(pair - step + pairs, pairs)] = ref[...]
    hidden = hidden_ref[...].reshape(count, query_ref.shape[1])
    column_ref[...] = nn(hidden, projection_ref[...]).astype(BF16)
    dense = nt(column_ref[...], query_ref[...]) * scale
    column_iota = lax.broadcasted_iota(jnp.int32, (groups, count), 1)
    places = jnp.zeros((groups, count), F32)
    lists = lists_ref[...]
    for c in range(size):
        places = places + jnp.where(lists[:, c : c + 1] == column_iota, float(c + 1), 0.0)
    group_iota = lax.broadcasted_iota(jnp.int32, (groups, rows), 0)
    mine = (group_iota == group_ref[...]).astype(F32).astype(BF16)
    place = tn(places.astype(BF16), mine)
    member = place > 0.5
    top = jnp.max(jnp.where(member, dense, -jnp.inf), axis=0, keepdims=True)
    power = jnp.where(member, jnp.exp(jnp.where(member, dense - top, 0.0)), 0.0)
    power_ref[...] = power
    place_ref[...] = place
    stat_ref[0:1, :] = top
    stat_ref[1:2, :] = jnp.sum(power, axis=0, keepdims=True)


def totals(stat_refs, owners, source):
    group_ref = stat_refs[source]
    tops = [group_ref[2 * owners : 2 * owners + 1, :]]
    sums = [group_ref[2 * owners + 1 : 2 * owners + 2, :]]
    for step, ref in enumerate(stat_refs):
        slot = (source - step) % owners
        tops.append(ref[2 * slot : 2 * slot + 1, :])
        sums.append(ref[2 * slot + 1 : 2 * slot + 2, :])
    top = functools.reduce(jnp.maximum, tops)
    total = functools.reduce(jnp.add, [s * jnp.exp(t - top) for s, t in zip(sums, tops)])
    return top, total


def soft_kernel(owners, direct, scale, *refs):
    power_ref, place_ref, label_ref, query_ref, column_ref, own_term_ref = refs[:6]
    stat_refs = refs[6 : 6 + owners]
    keep_ref, give_ref, sum_ref, factor_ref = refs[6 + owners :]
    rows = query_ref.shape[0]
    top, total = totals(stat_refs, owners, 0)
    place = place_ref[...]
    target = (place == (label_ref[...] + 1).astype(F32)).astype(F32)
    group_top = stat_refs[0][2 * owners : 2 * owners + 1, :]
    likely = power_ref[...] * jnp.exp(group_top - top) / total
    grad = jnp.where(place > 0.5, likely - target, 0.0)
    kept, _, size, _ = halves = (keep_ref.shape[0], 2, keep_ref.shape[1], rows)
    even, odd = grad.reshape(halves)[:, 0], grad.reshape(halves)[:, 1]
    first = lax.rem(lax.axis_index("pa"), 2) == 0
    mine = jnp.where(first, even, odd).reshape(kept * size, rows).astype(BF16)
    other = jnp.where(first, odd, even).reshape(kept * size, rows).astype(BF16)
    give_ref[...] = (nn(other, query_ref[...]) * scale).astype(BF16)
    keep_ref[...] = (nn(mine, query_ref[...]) * scale).reshape(keep_ref.shape)
    tops = [stat_refs[(owners - k) % owners][2 * k : 2 * k + 1, :] for k in range(owners)]
    tops = tops[: direct + 1] + [functools.reduce(jnp.maximum, tops[direct + 1 :])]
    factor = [jnp.exp(one - top) / total for one in tops]
    factor = jnp.concatenate(factor + [jnp.zeros((rows - direct - 2, rows), F32)], axis=0).T
    factor_ref[...] = factor
    own = factor[:, :1] * own_term_ref[...].astype(F32)
    sum_ref[...] = tn(grad.astype(BF16), column_ref[...]) + own


def merge_kernel(keep_ref, got_ref, own_ref, *outs):
    pairs = keep_ref.shape[0]
    pair = lax.div(lax.axis_index("pa"), 2)
    own_ref[...] = keep_ref[pair] + got_ref[pair].astype(F32)
    for step in range(1, pairs):
        to = lax.rem(pair + step, pairs)
        outs[step - 1][...] = (keep_ref[to] + got_ref[to].astype(F32)).astype(BF16)


def pool_kernel(owners, scale, *refs):
    stat_refs = refs[:owners]
    weight_refs = refs[owners : 2 * owners]
    turned_refs = refs[2 * owners : 3 * owners]
    out_ref = refs[3 * owners]
    acc = None
    for source in range(owners):
        top, total = totals(stat_refs, owners, source)
        factor = jnp.exp(stat_refs[0][2 * source : 2 * source + 1, :] - top) / total
        part = nn((weight_refs[source][...] * factor).astype(BF16), turned_refs[source][...])
        acc = part if acc is None else acc + part
    out_ref[...] = (acc * scale).astype(BF16)


def batch_kernel(projection_ref, own_ref, *refs):
    total = own_ref[...]
    for ref in refs[:-1]:
        total = total + ref[...].astype(F32)
    refs[-1][...] = nt(total.astype(BF16), projection_ref[...]).astype(BF16)


def query_kernel(scale, sum_ref, factor_ref, *refs):
    out_ref = refs[-1]
    total = sum_ref[...]
    for k, ref in enumerate(refs[:-1]):
        total = total + factor_ref[:, k + 1 : k + 2] * ref[...].astype(F32)
    out_ref[...] = (total * scale).astype(BF16)


def call(kernel, outs, arrays, after=(), flops=0, in_place=(), scratch=()):
    outs = [jax.ShapeDtypeStruct(*one) for one in outs]
    arrays = list(arrays) + list(in_place)
    moved = sum(a.size * a.dtype.itemsize for a in arrays + outs)
    count, waits = len(arrays), len(after)
    vmem = pl.BlockSpec(memory_space=pltpu.VMEM)

    def body(*refs):
        kernel(*refs[:count], *refs[count + waits :])

    results = pl.pallas_call(
        body,
        out_shape=outs,
        in_specs=[vmem] * (len(arrays) - len(in_place))
        + [pl.BlockSpec(memory_space=pltpu.HBM)] * len(in_place)
        + [pl.BlockSpec(memory_space=pl.ANY)] * waits,
        out_specs=[vmem] * len(outs),
        scratch_shapes=list(scratch),
        compiler_params=pltpu.CompilerParams(vmem_limit_bytes=VMEM_LIMIT),
        cost_estimate=pl.CostEstimate(flops=flops, bytes_accessed=moved, transcendentals=0),
    )(*arrays, *after)
    return list(results)


def shards(
    queries, batch_hidden, pool_hidden, projection, hard_ids, query_group, labels, group_lists
):
    rows, depth = queries.shape
    scale = 1.0 / math.sqrt(depth)
    owners = lax.axis_size("pb")
    pool_count = pool_hidden.shape[0]
    per = hard_ids.shape[1] // owners
    column_count = batch_hidden.shape[0] * lax.axis_size("pa")
    members, size = lax.axis_size("pa"), batch_hidden.shape[0]
    pairs = members // 2
    term, weight = ((rows, depth), BF16), ((pool_count, rows), F32)

    ring = [0] + list(range(1, owners, 2)) + list(range(2, owners, 2))[::-1]

    def shift(x, k):
        to = [(ring[p], ring[(p + k) % owners]) for p in range(owners)]
        return lax.ppermute(x, "pb", to)

    def hold(x, others):
        return lax.optimization_barrier([x] + list(others))[0]

    def swap(x):
        return lax.ppermute(x, "pa", [(i, i ^ 1) for i in range(members)])

    def pass_on(x, step):
        return lax.ppermute(x, "pa", [(i, (i + 2 * step) % members) for i in range(members)])

    (packed,) = call(
        functools.partial(pack_kernel, owners, pool_count),
        [((rows + SUB, depth), BF16)],
        [hard_ids.T],
        in_place=[queries],
        scratch=[pltpu.SemaphoreType.DMA],
    )
    block = shift(packed, 1)
    other = swap(batch_hidden)
    table, turned, own_stat, own_weight, own_term = call(
        functools.partial(own_kernel, owners, per, scale),
        [((pool_count, depth), BF16), term, ((2, rows), F32), weight, term],
        [packed, pool_hidden, projection],
        flops=2 * depth * (pool_count * depth + rows * depth + 2 * rows * pool_count),
    )
    (chip,) = call(pair_kernel, [((2, size, depth), BF16)], [batch_hidden, other], flops=size * depth)
    column, power, place, group_stat = call(
        functools.partial(group_kernel, scale, pairs),
        [
            ((column_count, depth), BF16),
            ((column_count, rows), F32),
            ((column_count, rows), F32),
            ((2, rows), F32),
        ],
        [queries, projection, query_group[None, :], group_lists]
        + [chip]
        + [pass_on(chip, step) for step in range(1, pairs)],
        scratch=[pltpu.VMEM((pairs, 2, size, depth), BF16)],
        flops=2 * depth * column_count * (rows + depth),
    )
    stats, weights, terms, turned = [own_stat], [own_weight], [], [turned]
    direct = owners // 2 - 1
    waits, chain = [own_stat, chip], None
    for slot in range(1, owners):
        last = slot + 1 == owners
        later = None if last else shift(hold(block, waits), 1)
        one_stat, one_weight = call(
            functools.partial(score_kernel, owners, per, scale),
            [((2, rows), F32), weight],
            [table, block],
            after=turned[1:] if last else (),
            flops=2 * rows * pool_count * depth,
        )
        stats.append(one_stat)
        weights.append(one_weight)
        if last:
            (stat,) = call(
                join_kernel, [((2 * owners + 2, rows), F32)], stats + [group_stat], flops=rows
            )
        straight = slot <= direct or last
        shape = ((rows, depth), BF16) if straight else ((rows + SUB, depth), BF16)
        (one_term,) = call(
            term_kernel,
            [shape],
            [table, one_stat, one_weight] + ([] if chain is None else [chain]),
            flops=2 * rows * pool_count * depth,
        )
        if slot <= direct:
            terms.append((slot, one_term))
        else:
            chain = (slot, one_term)
            if not last:
                chain = shift(one_term, 1)
        turned += call(
            functools.partial(turn_kernel, 1),
            [term],
            [projection, block],
            after=[stat if last else one_stat],
            flops=2 * rows * depth * depth,
        )
        waits = [one_stat, group_stat]
        block = later
    stats = [stat]
    for k in range(1, owners):
        stats.append(shift(stat, k))
    terms = [shift(hold(one, [stat]), owners - k) for k, one in terms + [chain]]
    keep, give, total, factor = call(
        functools.partial(soft_kernel, owners, direct, scale),
        [
            ((pairs, size, depth), F32),
            ((pairs * size, depth), BF16),
            ((rows, depth), F32),
            ((rows, rows), F32),
        ],
        [power, place, labels[None, :], queries, column, own_term] + stats,
        after=turned[-1:],
        flops=4 * rows * column_count * depth,
    )
    got = swap(give)
    parts = call(
        merge_kernel,
        [((size, depth), F32)] + [((size, depth), BF16)] * (pairs - 1),
        [keep, got.reshape(pairs, size, depth)],
        flops=column_count * depth,
    )
    for step in range(1, pairs):
        parts[step] = pass_on(parts[step], step)
    (pool_hidden_grad,) = call(
        functools.partial(pool_kernel, owners, scale),
        [((pool_count, depth), BF16)],
        stats + weights + turned,
        flops=2 * rows * owners * pool_count * depth,
    )
    (batch_hidden_grad,) = call(
        batch_kernel,
        [(batch_hidden.shape, BF16)],
        [projection] + parts,
        flops=2 * batch_hidden.shape[0] * depth * depth,
    )
    (query_grad,) = call(
        functools.partial(query_kernel, scale),
        [((rows, depth), BF16)],
        [total, factor] + terms,
        flops=4 * rows * depth * owners,
    )
    return (query_grad, batch_hidden_grad, pool_hidden_grad)


def solution(mesh):
    spread = P(("pa", "pb"))
    return jax.shard_map(
        shards,
        mesh=mesh,
        in_specs=(spread, spread, spread, P(), spread, spread, spread, P()),
        out_specs=(spread, spread, spread),
        check_vma=False,
    )
```

```python
import functools
import math

import jax
import jax.numpy as jnp
from jax import lax
from jax.experimental import pallas as pl
from jax.experimental.pallas import tpu as pltpu
from jax.sharding import PartitionSpec as P


F32 = jnp.float32
BF16 = jnp.bfloat16
LOW_BITS = 4
SUB = 8
VMEM_LIMIT = 8 << 20


def nn(a, b):
    return lax.dot_general(a, b, (((1,), (0,)), ((), ())), preferred_element_type=F32)


def nt(a, b):
    return lax.dot_general(a, b, (((1,), (1,)), ((), ())), preferred_element_type=F32)


def tn(a, b):
    return lax.dot_general(a, b, (((0,), (0,)), ((), ())), preferred_element_type=F32)


def pack_kernel(owners, pool_count, ids_hbm, query_ref, packed_ref, sem, ids_ref, ids_sem):
    rows, depth = query_ref.shape
    hard_count = ids_ref.shape[0]
    per = hard_count // owners
    copy = pltpu.make_async_copy(query_ref, packed_ref.at[:rows, :], sem)
    ids_copy = pltpu.make_async_copy(ids_hbm, ids_ref, ids_sem)
    ids_copy.start()
    copy.start()
    ids_copy.wait()
    packed_ref[rows:, :] = jnp.zeros((SUB, depth), BF16)
    for block in range(hard_count // SUB):
        lines = []
        for place in range(block * SUB, (block + 1) * SUB):
            owner, j = divmod(place, per)
            k = j * owners + owner
            lines.append(ids_ref[k : k + 1, :] - owner * pool_count)
        ids = jnp.concatenate(lines, axis=0)
        high = jnp.right_shift(ids, LOW_BITS)
        low = ids - jnp.left_shift(high, LOW_BITS)
        start = 2 * block * rows
        packed_ref[rows:, start : start + rows] = high.astype(F32).astype(BF16)
        packed_ref[rows:, start + rows : start + 2 * rows] = low.astype(F32).astype(BF16)
    copy.wait()


def local_ids(packed_ref, me, rows, owners, per):
    found = None
    for owner in range(owners):
        parts = []
        for j in range(per):
            block, sub = divmod(owner * per + j, SUB)
            start = 2 * block * rows
            high = packed_ref[rows:, start : start + rows].astype(F32)
            low = packed_ref[rows:, start + rows : start + 2 * rows].astype(F32)
            ids = high * float(1 << LOW_BITS) + low
            parts.append(ids[sub : sub + 1, :])
        if found is None:
            found = parts
        else:
            found = [jnp.where(me == owner, new, old) for new, old in zip(parts, found)]
    return found


def score_block(me, packed_ref, table_ref, rows, owners, per, scale):
    count = table_ref.shape[0]
    ids = local_ids(packed_ref, me, rows, owners, per)
    dense = nt(table_ref[...], packed_ref[:rows, :])
    row_iota = lax.broadcasted_iota(jnp.int32, (count, rows), 0).astype(F32)
    hits = [row_iota == one for one in ids]
    scores = [jnp.sum(jnp.where(hit, dense, 0.0), axis=0, keepdims=True) * scale for hit in hits]
    top = functools.reduce(jnp.maximum, scores)
    powers = [jnp.exp(one - top) for one in scores]
    weight = jnp.zeros((count, rows), F32)
    for hit, one in zip(hits, powers):
        weight = weight + jnp.where(hit, one, 0.0)
    return weight, top, functools.reduce(jnp.add, powers)


def own_kernel(owners, per, scale, packed_ref, hidden_ref, projection_ref, *outs):
    table_ref, turned_ref, stat_ref, weight_ref, term_ref = outs
    me = lax.axis_index("pb")
    rows = packed_ref.shape[0] - SUB
    table_ref[...] = nn(hidden_ref[...], projection_ref[...]).astype(BF16)
    turned_ref[...] = nt(packed_ref[:rows, :], projection_ref[...]).astype(BF16)
    weight, top, total = score_block(me, packed_ref, table_ref, rows, owners, per, scale)
    stat_ref[0:1, :] = top
    stat_ref[1:2, :] = total
    weight_ref[...] = weight
    term_ref[...] = tn(weight.astype(BF16), table_ref[...]).astype(BF16)


def score_kernel(owners, per, scale, table_ref, packed_ref, stat_ref, weight_ref):
    rows = packed_ref.shape[0] - SUB
    me = lax.axis_index("pb")
    weight, top, total = score_block(me, packed_ref, table_ref, rows, owners, per, scale)
    stat_ref[0:1, :] = top
    stat_ref[1:2, :] = total
    weight_ref[...] = weight


def term_kernel(table_ref, stat_ref, weight_ref, *refs):
    old_ref, out_ref = refs if len(refs) == 2 else (None, refs[0])
    weight, top = weight_ref[...], stat_ref[0:1, :]
    rows = weight.shape[1]
    if old_ref is not None:
        parts = [old_ref[rows:, k * rows : (k + 1) * rows].astype(F32)[0:1, :] for k in range(3)]
        before = parts[0] + parts[1] + parts[2]
        both = jnp.maximum(before, top)
        weight = weight * jnp.exp(top - both)
        column = jnp.broadcast_to(jnp.exp(before - both), (rows, rows)).T[:, :1]
        top = both
    term = tn(weight.astype(BF16), table_ref[...])
    if old_ref is not None:
        term = term + column * old_ref[:rows, :].astype(F32)
    out_ref[:rows, :] = term.astype(BF16)
    if out_ref.shape[0] > rows:
        out_ref[rows:, :] = jnp.zeros((SUB, out_ref.shape[1]), BF16)
        left = jnp.broadcast_to(top, (SUB, rows))
        for k in range(3):
            part = left.astype(BF16)
            out_ref[rows:, k * rows : (k + 1) * rows] = part
            left = left - part.astype(F32)


def join_kernel(*refs):
    for k, ref in enumerate(refs[:-1]):
        refs[-1][2 * k : 2 * k + 2, :] = ref[...]


def pair_kernel(mine_ref, other_ref, out_ref):
    first = lax.rem(lax.axis_index("pa"), 2) == 0
    mine, other = mine_ref[...], other_ref[...]
    out_ref[0] = jnp.where(first, mine, other)
    out_ref[1] = jnp.where(first, other, mine)


def turn_kernel(count, projection_ref, *refs):
    for packed_ref, out_ref in zip(refs[:count], refs[-count:]):
        rows = out_ref.shape[0]
        out_ref[...] = nt(packed_ref[:rows, :], projection_ref[...]).astype(BF16)


def group_kernel(scale, pairs, query_ref, projection_ref, group_ref, lists_ref, *refs):
    column_ref, power_ref, place_ref, stat_ref, hidden_ref = refs[pairs:]
    rows = query_ref.shape[0]
    groups, size = lists_ref.shape
    count = column_ref.shape[0]
    pair = lax.div(lax.axis_index("pa"), 2)
    for step, ref in enumerate(refs[:pairs]):
        hidden_ref[lax.rem(pair - step + pairs, pairs)] = ref[...]
    hidden = hidden_ref[...].reshape(count, query_ref.shape[1])
    column_ref[...] = nn(hidden, projection_ref[...]).astype(BF16)
    dense = nt(column_ref[...], query_ref[...]) * scale
    column_iota = lax.broadcasted_iota(jnp.int32, (groups, count), 1)
    places = jnp.zeros((groups, count), F32)
    lists = lists_ref[...]
    for c in range(size):
        places = places + jnp.where(lists[:, c : c + 1] == column_iota, float(c + 1), 0.0)
    group_iota = lax.broadcasted_iota(jnp.int32, (groups, rows), 0)
    mine = (group_iota == group_ref[...]).astype(F32).astype(BF16)
    place = tn(places.astype(BF16), mine)
    member = place > 0.5
    top = jnp.max(jnp.where(member, dense, -jnp.inf), axis=0, keepdims=True)
    power = jnp.where(member, jnp.exp(jnp.where(member, dense - top, 0.0)), 0.0)
    power_ref[...] = power
    place_ref[...] = place
    stat_ref[0:1, :] = top
    stat_ref[1:2, :] = jnp.sum(power, axis=0, keepdims=True)


def totals(stat_refs, owners, source):
    group_ref = stat_refs[source]
    tops = [group_ref[2 * owners : 2 * owners + 1, :]]
    sums = [group_ref[2 * owners + 1 : 2 * owners + 2, :]]
    for step, ref in enumerate(stat_refs):
        slot = (source - step) % owners
        tops.append(ref[2 * slot : 2 * slot + 1, :])
        sums.append(ref[2 * slot + 1 : 2 * slot + 2, :])
    top = functools.reduce(jnp.maximum, tops)
    total = functools.reduce(jnp.add, [s * jnp.exp(t - top) for s, t in zip(sums, tops)])
    return top, total


def soft_kernel(owners, direct, scale, *refs):
    power_ref, place_ref, label_ref, query_ref, column_ref, own_term_ref = refs[:6]
    stat_refs = refs[6 : 6 + owners]
    keep_ref, give_ref, sum_ref, factor_ref = refs[6 + owners :]
    rows = query_ref.shape[0]
    top, total = totals(stat_refs, owners, 0)
    place = place_ref[...]
    target = (place == (label_ref[...] + 1).astype(F32)).astype(F32)
    group_top = stat_refs[0][2 * owners : 2 * owners + 1, :]
    likely = power_ref[...] * jnp.exp(group_top - top) / total
    grad = jnp.where(place > 0.5, likely - target, 0.0)
    kept, _, size, _ = halves = (keep_ref.shape[0], 2, keep_ref.shape[1], rows)
    even, odd = grad.reshape(halves)[:, 0], grad.reshape(halves)[:, 1]
    first = lax.rem(lax.axis_index("pa"), 2) == 0
    mine = jnp.where(first, even, odd).reshape(kept * size, rows).astype(BF16)
    other = jnp.where(first, odd, even).reshape(kept * size, rows).astype(BF16)
    give_ref[...] = (nn(other, query_ref[...]) * scale).astype(BF16)
    keep_ref[...] = (nn(mine, query_ref[...]) * scale).reshape(keep_ref.shape)
    tops = [stat_refs[(owners - k) % owners][2 * k : 2 * k + 1, :] for k in range(owners)]
    tops = tops[: direct + 1] + [functools.reduce(jnp.maximum, tops[direct + 1 :])]
    factor = [jnp.exp(one - top) / total for one in tops]
    factor = jnp.concatenate(factor + [jnp.zeros((rows - direct - 2, rows), F32)], axis=0).T
    factor_ref[...] = factor
    own = factor[:, :1] * own_term_ref[...].astype(F32)
    sum_ref[...] = tn(grad.astype(BF16), column_ref[...]) + own


def merge_kernel(keep_ref, got_ref, own_ref, *outs):
    pairs = keep_ref.shape[0]
    pair = lax.div(lax.axis_index("pa"), 2)
    own_ref[...] = keep_ref[pair] + got_ref[pair].astype(F32)
    for step in range(1, pairs):
        to = lax.rem(pair + step, pairs)
        outs[step - 1][...] = (keep_ref[to] + got_ref[to].astype(F32)).astype(BF16)


def pool_kernel(owners, scale, *refs):
    stat_refs = refs[:owners]
    weight_refs = refs[owners : 2 * owners]
    turned_refs = refs[2 * owners : 3 * owners]
    out_ref = refs[3 * owners]
    acc = None
    for source in range(owners):
        top, total = totals(stat_refs, owners, source)
        factor = jnp.exp(stat_refs[0][2 * source : 2 * source + 1, :] - top) / total
        part = nn((weight_refs[source][...] * factor).astype(BF16), turned_refs[source][...])
        acc = part if acc is None else acc + part
    out_ref[...] = (acc * scale).astype(BF16)


def batch_kernel(projection_ref, own_ref, *refs):
    total = own_ref[...]
    for ref in refs[:-1]:
        total = total + ref[...].astype(F32)
    refs[-1][...] = nt(total.astype(BF16), projection_ref[...]).astype(BF16)


def query_kernel(scale, sum_ref, factor_ref, *refs):
    out_ref = refs[-1]
    total = sum_ref[...]
    for k, ref in enumerate(refs[:-1]):
        total = total + factor_ref[:, k + 1 : k + 2] * ref[...].astype(F32)
    out_ref[...] = (total * scale).astype(BF16)


def call(kernel, outs, arrays, after=(), flops=0, in_place=(), scratch=()):
    outs = [jax.ShapeDtypeStruct(*one) for one in outs]
    arrays = list(arrays) + list(in_place)
    moved = sum(a.size * a.dtype.itemsize for a in arrays + outs)
    count, waits = len(arrays), len(after)
    vmem = pl.BlockSpec(memory_space=pltpu.VMEM)

    def body(*refs):
        kernel(*refs[:count], *refs[count + waits :])

    results = pl.pallas_call(
        body,
        out_shape=outs,
        in_specs=[vmem] * (len(arrays) - len(in_place))
        + [pl.BlockSpec(memory_space=pltpu.HBM)] * len(in_place)
        + [pl.BlockSpec(memory_space=pl.ANY)] * waits,
        out_specs=[vmem] * len(outs),
        scratch_shapes=list(scratch),
        compiler_params=pltpu.CompilerParams(vmem_limit_bytes=VMEM_LIMIT),
        cost_estimate=pl.CostEstimate(flops=flops, bytes_accessed=moved, transcendentals=0),
    )(*arrays, *after)
    return list(results)


def shards(
    queries, batch_hidden, pool_hidden, projection, hard_ids, query_group, labels, group_lists
):
    rows, depth = queries.shape
    scale = 1.0 / math.sqrt(depth)
    owners = lax.axis_size("pb")
    pool_count = pool_hidden.shape[0]
    per = hard_ids.shape[1] // owners
    column_count = batch_hidden.shape[0] * lax.axis_size("pa")
    members, size = lax.axis_size("pa"), batch_hidden.shape[0]
    pairs = members // 2
    term, weight = ((rows, depth), BF16), ((pool_count, rows), F32)

    ring = [0] + list(range(1, owners, 2)) + list(range(2, owners, 2))[::-1]

    def shift(x, k):
        to = [(ring[p], ring[(p + k) % owners]) for p in range(owners)]
        return lax.ppermute(x, "pb", to)

    def hold(x, others):
        return lax.optimization_barrier([x] + list(others))[0]

    def swap(x):
        return lax.ppermute(x, "pa", [(i, i ^ 1) for i in range(members)])

    def pass_on(x, step):
        return lax.ppermute(x, "pa", [(i, (i + 2 * step) % members) for i in range(members)])

    (packed,) = call(
        functools.partial(pack_kernel, owners, pool_count),
        [((rows + SUB, depth), BF16)],
        [],
        in_place=[
            pltpu.with_memory_space_constraint(hard_ids.T, pltpu.HBM),
            pltpu.with_memory_space_constraint(queries, pltpu.HBM),
        ],
        scratch=[
            pltpu.SemaphoreType.DMA,
            pltpu.VMEM(hard_ids.shape[::-1], jnp.int32),
            pltpu.SemaphoreType.DMA,
        ],
    )
    block = shift(packed, 1)
    other = swap(batch_hidden)
    table, turned, own_stat, own_weight, own_term = call(
        functools.partial(own_kernel, owners, per, scale),
        [((pool_count, depth), BF16), term, ((2, rows), F32), weight, term],
        [packed, pool_hidden, projection],
        flops=2 * depth * (pool_count * depth + rows * depth + 2 * rows * pool_count),
    )
    (chip,) = call(pair_kernel, [((2, size, depth), BF16)], [batch_hidden, other], flops=size * depth)
    chips = [chip] + [pass_on(chip, step) for step in range(1, pairs)]
    column, power, place, group_stat = call(
        functools.partial(group_kernel, scale, pairs),
        [
            ((column_count, depth), BF16),
            ((column_count, rows), F32),
            ((column_count, rows), F32),
            ((2, rows), F32),
        ],
        [queries, projection, query_group[None, :], group_lists] + chips,
        scratch=[pltpu.VMEM((pairs, 2, size, depth), BF16)],
        flops=2 * depth * column_count * (rows + depth),
    )
    stats, weights, terms, turned = [own_stat], [own_weight], [], [turned]
    direct = owners // 2 - 1
    waits, chain = [own_stat, chip], None
    for slot in range(1, owners):
        last = slot + 1 == owners
        later = None if last else shift(hold(block, waits), 1)
        one_stat, one_weight = call(
            functools.partial(score_kernel, owners, per, scale),
            [((2, rows), F32), weight],
            [table, block],
            after=turned[1:] if last else (),
            flops=2 * rows * pool_count * depth,
        )
        stats.append(one_stat)
        weights.append(one_weight)
        if last:
            (stat,) = call(
                join_kernel, [((2 * owners + 2, rows), F32)], stats + [group_stat], flops=rows
            )
        straight = slot <= direct or last
        shape = ((rows, depth), BF16) if straight else ((rows + SUB, depth), BF16)
        (one_term,) = call(
            term_kernel,
            [shape],
            [table, one_stat, one_weight] + ([] if chain is None else [chain]),
            flops=2 * rows * pool_count * depth,
        )
        if slot <= direct:
            terms.append((slot, one_term))
        else:
            chain = (slot, one_term)
            if not last:
                chain = shift(one_term, 1)
        turned += call(
            functools.partial(turn_kernel, 1),
            [term],
            [projection, block],
            after=[stat if last else one_stat],
            flops=2 * rows * depth * depth,
        )
        waits = [one_stat]
        block = later
    stats = [stat]
    for k in range(1, owners):
        stats.append(shift(stat, k))
    back = []
    for k, one in terms + [chain]:
        back.append(shift(hold(one, [stat]) if k <= direct else one, owners - k))
    terms = back
    keep, give, total, factor = call(
        functools.partial(soft_kernel, owners, direct, scale),
        [
            ((pairs, size, depth), F32),
            ((pairs * size, depth), BF16),
            ((rows, depth), F32),
            ((rows, rows), F32),
        ],
        [power, place, labels[None, :], queries, column, own_term] + stats,
        after=turned[-1:],
        flops=4 * rows * column_count * depth,
    )
    got = swap(give)
    parts = call(
        merge_kernel,
        [((size, depth), F32)] + [((size, depth), BF16)] * (pairs - 1),
        [keep, got.reshape(pairs, size, depth)],
        flops=column_count * depth,
    )
    for step in range(1, pairs):
        parts[step] = pass_on(parts[step], step)
    (pool_hidden_grad,) = call(
        functools.partial(pool_kernel, owners, scale),
        [((pool_count, depth), BF16)],
        stats + weights + turned,
        flops=2 * rows * owners * pool_count * depth,
    )
    (batch_hidden_grad,) = call(
        batch_kernel,
        [(batch_hidden.shape, BF16)],
        [projection] + parts,
        flops=2 * batch_hidden.shape[0] * depth * depth,
    )
    (query_grad,) = call(
        functools.partial(query_kernel, scale),
        [((rows, depth), BF16)],
        [total, factor] + terms,
        flops=4 * rows * depth * owners,
    )
    return (query_grad, batch_hidden_grad, pool_hidden_grad)


def solution(mesh):
    spread = P(("pa", "pb"))
    return jax.shard_map(
        shards,
        mesh=mesh,
        in_specs=(spread, spread, spread, P(), spread, spread, spread, P()),
        out_specs=(spread, spread, spread),
        check_vma=False,
    )
```

```python
import functools
import math

import jax
import jax.numpy as jnp
from jax import lax
from jax.experimental import pallas as pl
from jax.experimental.pallas import tpu as pltpu
from jax.sharding import PartitionSpec as P


F32 = jnp.float32
BF16 = jnp.bfloat16
LOW_BITS = 4
SUB = 8
VMEM_LIMIT = 8 << 20


def nn(a, b):
    return lax.dot_general(a, b, (((1,), (0,)), ((), ())), preferred_element_type=F32)


def nt(a, b):
    return lax.dot_general(a, b, (((1,), (1,)), ((), ())), preferred_element_type=F32)


def tn(a, b):
    return lax.dot_general(a, b, (((0,), (0,)), ((), ())), preferred_element_type=F32)


def pack_kernel(owners, pool_count, ids_hbm, query_ref, packed_ref, sem, ids_ref, ids_sem):
    rows, depth = query_ref.shape
    hard_count = ids_ref.shape[0]
    per = hard_count // owners
    copy = pltpu.make_async_copy(query_ref, packed_ref.at[:rows, :], sem)
    ids_copy = pltpu.make_async_copy(ids_hbm, ids_ref, ids_sem)
    ids_copy.start()
    copy.start()
    ids_copy.wait()
    packed_ref[rows:, :] = jnp.zeros((SUB, depth), BF16)
    for block in range(hard_count // SUB):
        lines = []
        for place in range(block * SUB, (block + 1) * SUB):
            owner, j = divmod(place, per)
            k = j * owners + owner
            lines.append(ids_ref[k : k + 1, :] - owner * pool_count)
        ids = jnp.concatenate(lines, axis=0)
        high = jnp.right_shift(ids, LOW_BITS)
        low = ids - jnp.left_shift(high, LOW_BITS)
        start = 2 * block * rows
        packed_ref[rows:, start : start + rows] = high.astype(F32).astype(BF16)
        packed_ref[rows:, start + rows : start + 2 * rows] = low.astype(F32).astype(BF16)
    copy.wait()


def local_ids(packed_ref, me, rows, owners, per):
    found = None
    for owner in range(owners):
        parts = []
        for j in range(per):
            block, sub = divmod(owner * per + j, SUB)
            start = 2 * block * rows
            high = packed_ref[rows:, start : start + rows].astype(F32)
            low = packed_ref[rows:, start + rows : start + 2 * rows].astype(F32)
            ids = high * float(1 << LOW_BITS) + low
            parts.append(ids[sub : sub + 1, :])
        if found is None:
            found = parts
        else:
            found = [jnp.where(me == owner, new, old) for new, old in zip(parts, found)]
    return found


def score_block(me, packed_ref, table_ref, rows, owners, per, scale):
    count = table_ref.shape[0]
    ids = local_ids(packed_ref, me, rows, owners, per)
    dense = nt(table_ref[...], packed_ref[:rows, :])
    row_iota = lax.broadcasted_iota(jnp.int32, (count, rows), 0).astype(F32)
    hits = [row_iota == one for one in ids]
    scores = [jnp.sum(jnp.where(hit, dense, 0.0), axis=0, keepdims=True) * scale for hit in hits]
    top = functools.reduce(jnp.maximum, scores)
    powers = [jnp.exp(one - top) for one in scores]
    weight = jnp.zeros((count, rows), F32)
    for hit, one in zip(hits, powers):
        weight = weight + jnp.where(hit, one, 0.0)
    return weight, top, functools.reduce(jnp.add, powers)


def own_kernel(owners, per, scale, packed_ref, hidden_ref, projection_ref, *outs):
    table_ref, turned_ref, stat_ref, weight_ref, term_ref = outs
    me = lax.axis_index("pb")
    rows = packed_ref.shape[0] - SUB
    table_ref[...] = nn(hidden_ref[...], projection_ref[...]).astype(BF16)
    turned_ref[...] = nt(packed_ref[:rows, :], projection_ref[...]).astype(BF16)
    weight, top, total = score_block(me, packed_ref, table_ref, rows, owners, per, scale)
    stat_ref[0:1, :] = top
    stat_ref[1:2, :] = total
    weight_ref[...] = weight
    term_ref[...] = tn(weight.astype(BF16), table_ref[...]).astype(BF16)


def score_kernel(owners, per, scale, table_ref, packed_ref, stat_ref, weight_ref):
    rows = packed_ref.shape[0] - SUB
    me = lax.axis_index("pb")
    weight, top, total = score_block(me, packed_ref, table_ref, rows, owners, per, scale)
    stat_ref[0:1, :] = top
    stat_ref[1:2, :] = total
    weight_ref[...] = weight


def term_kernel(table_ref, stat_ref, weight_ref, *refs):
    old_ref, out_ref = refs if len(refs) == 2 else (None, refs[0])
    weight, top = weight_ref[...], stat_ref[0:1, :]
    rows = weight.shape[1]
    if old_ref is not None:
        parts = [old_ref[rows:, k * rows : (k + 1) * rows].astype(F32)[0:1, :] for k in range(3)]
        before = parts[0] + parts[1] + parts[2]
        both = jnp.maximum(before, top)
        weight = weight * jnp.exp(top - both)
        column = jnp.broadcast_to(jnp.exp(before - both), (rows, rows)).T[:, :1]
        top = both
    term = tn(weight.astype(BF16), table_ref[...])
    if old_ref is not None:
        term = term + column * old_ref[:rows, :].astype(F32)
    out_ref[:rows, :] = term.astype(BF16)
    if out_ref.shape[0] > rows:
        out_ref[rows:, :] = jnp.zeros((SUB, out_ref.shape[1]), BF16)
        left = jnp.broadcast_to(top, (SUB, rows))
        for k in range(3):
            part = left.astype(BF16)
            out_ref[rows:, k * rows : (k + 1) * rows] = part
            left = left - part.astype(F32)


def join_kernel(*refs):
    for k, ref in enumerate(refs[:-1]):
        refs[-1][2 * k : 2 * k + 2, :] = ref[...]


def pair_kernel(mine_ref, other_ref, out_ref):
    first = lax.rem(lax.axis_index("pa"), 2) == 0
    mine, other = mine_ref[...], other_ref[...]
    out_ref[0] = jnp.where(first, mine, other)
    out_ref[1] = jnp.where(first, other, mine)


def turn_kernel(count, projection_ref, *refs):
    for packed_ref, out_ref in zip(refs[:count], refs[-count:]):
        rows = out_ref.shape[0]
        out_ref[...] = nt(packed_ref[:rows, :], projection_ref[...]).astype(BF16)


def group_kernel(scale, pairs, query_ref, projection_ref, group_ref, lists_ref, *refs):
    column_ref, power_ref, place_ref, stat_ref, hidden_ref = refs[pairs:]
    rows = query_ref.shape[0]
    groups, size = lists_ref.shape
    count = column_ref.shape[0]
    pair = lax.div(lax.axis_index("pa"), 2)
    for step, ref in enumerate(refs[:pairs]):
        hidden_ref[lax.rem(pair - step + pairs, pairs)] = ref[...]
    hidden = hidden_ref[...].reshape(count, query_ref.shape[1])
    column_ref[...] = nn(hidden, projection_ref[...]).astype(BF16)
    dense = nt(column_ref[...], query_ref[...]) * scale
    column_iota = lax.broadcasted_iota(jnp.int32, (groups, count), 1)
    places = jnp.zeros((groups, count), F32)
    lists = lists_ref[...]
    for c in range(size):
        places = places + jnp.where(lists[:, c : c + 1] == column_iota, float(c + 1), 0.0)
    group_iota = lax.broadcasted_iota(jnp.int32, (groups, rows), 0)
    mine = (group_iota == group_ref[...]).astype(F32).astype(BF16)
    place = tn(places.astype(BF16), mine)
    member = place > 0.5
    top = jnp.max(jnp.where(member, dense, -jnp.inf), axis=0, keepdims=True)
    power = jnp.where(member, jnp.exp(jnp.where(member, dense - top, 0.0)), 0.0)
    power_ref[...] = power
    place_ref[...] = place
    stat_ref[0:1, :] = top
    stat_ref[1:2, :] = jnp.sum(power, axis=0, keepdims=True)


def totals(stat_refs, owners, source):
    group_ref = stat_refs[source]
    tops = [group_ref[2 * owners : 2 * owners + 1, :]]
    sums = [group_ref[2 * owners + 1 : 2 * owners + 2, :]]
    for step, ref in enumerate(stat_refs):
        slot = (source - step) % owners
        tops.append(ref[2 * slot : 2 * slot + 1, :])
        sums.append(ref[2 * slot + 1 : 2 * slot + 2, :])
    top = functools.reduce(jnp.maximum, tops)
    total = functools.reduce(jnp.add, [s * jnp.exp(t - top) for s, t in zip(sums, tops)])
    return top, total


def soft_kernel(owners, direct, scale, *refs):
    power_ref, place_ref, label_ref, turned_ref, column_ref, own_term_ref = refs[:6]
    stat_refs = refs[6 : 6 + owners]
    keep_ref, give_ref, sum_ref, factor_ref = refs[6 + owners :]
    rows = turned_ref.shape[0]
    top, total = totals(stat_refs, owners, 0)
    place = place_ref[...]
    target = (place == (label_ref[...] + 1).astype(F32)).astype(F32)
    group_top = stat_refs[0][2 * owners : 2 * owners + 1, :]
    likely = power_ref[...] * jnp.exp(group_top - top) / total
    grad = jnp.where(place > 0.5, likely - target, 0.0)
    kept, _, size, _ = halves = (keep_ref.shape[0], 2, keep_ref.shape[1], rows)
    even, odd = grad.reshape(halves)[:, 0], grad.reshape(halves)[:, 1]
    first = lax.rem(lax.axis_index("pa"), 2) == 0
    mine = jnp.where(first, even, odd).reshape(kept * size, rows).astype(BF16)
    other = jnp.where(first, odd, even).reshape(kept * size, rows).astype(BF16)
    give_ref[...] = (nn(other, turned_ref[...]) * scale).astype(BF16)
    keep_ref[...] = (nn(mine, turned_ref[...]) * scale).reshape(keep_ref.shape)
    tops = [stat_refs[(owners - k) % owners][2 * k : 2 * k + 1, :] for k in range(owners)]
    tops = tops[: direct + 1] + [functools.reduce(jnp.maximum, tops[direct + 1 :])]
    factor = [jnp.exp(one - top) / total for one in tops]
    factor = jnp.concatenate(factor + [jnp.zeros((rows - direct - 2, rows), F32)], axis=0).T
    factor_ref[...] = factor
    own = factor[:, :1] * own_term_ref[...].astype(F32)
    sum_ref[...] = tn(grad.astype(BF16), column_ref[...]) + own


def merge_kernel(keep_ref, got_ref, own_ref, *outs):
    pairs = keep_ref.shape[0]
    pair = lax.div(lax.axis_index("pa"), 2)
    own_ref[...] = keep_ref[pair] + got_ref[pair].astype(F32)
    for step in range(1, pairs):
        to = lax.rem(pair + step, pairs)
        outs[step - 1][...] = (keep_ref[to] + got_ref[to].astype(F32)).astype(BF16)


def pool_kernel(owners, scale, *refs):
    stat_refs = refs[:owners]
    weight_refs = refs[owners : 2 * owners]
    turned_refs = refs[2 * owners : 3 * owners]
    out_ref = refs[3 * owners]
    acc = None
    for source in range(owners):
        top, total = totals(stat_refs, owners, source)
        factor = jnp.exp(stat_refs[0][2 * source : 2 * source + 1, :] - top) / total
        part = nn((weight_refs[source][...] * factor).astype(BF16), turned_refs[source][...])
        acc = part if acc is None else acc + part
    out_ref[...] = (acc * scale).astype(BF16)


def last_kernel(scale, parts, sum_ref, factor_ref, *refs):
    query_ref, batch_ref = refs[-2:]
    batch_ref[...] = functools.reduce(
        jnp.add, [ref[...].astype(F32) for ref in refs[:parts]]
    ).astype(BF16)
    total = sum_ref[...]
    for k, ref in enumerate(refs[parts:-2]):
        total = total + factor_ref[:, k + 1 : k + 2] * ref[...].astype(F32)
    query_ref[...] = (total * scale).astype(BF16)


def call(kernel, outs, arrays, after=(), flops=0, in_place=(), scratch=()):
    outs = [jax.ShapeDtypeStruct(*one) for one in outs]
    arrays = list(arrays) + list(in_place)
    moved = sum(a.size * a.dtype.itemsize for a in arrays + outs)
    count, waits = len(arrays), len(after)
    vmem = pl.BlockSpec(memory_space=pltpu.VMEM)

    def body(*refs):
        kernel(*refs[:count], *refs[count + waits :])

    results = pl.pallas_call(
        body,
        out_shape=outs,
        in_specs=[vmem] * (len(arrays) - len(in_place))
        + [pl.BlockSpec(memory_space=pltpu.HBM)] * len(in_place)
        + [pl.BlockSpec(memory_space=pl.ANY)] * waits,
        out_specs=[vmem] * len(outs),
        scratch_shapes=list(scratch),
        compiler_params=pltpu.CompilerParams(vmem_limit_bytes=VMEM_LIMIT),
        cost_estimate=pl.CostEstimate(flops=flops, bytes_accessed=moved, transcendentals=0),
    )(*arrays, *after)
    return list(results)


def shards(
    queries, batch_hidden, pool_hidden, projection, hard_ids, query_group, labels, group_lists
):
    rows, depth = queries.shape
    scale = 1.0 / math.sqrt(depth)
    owners = lax.axis_size("pb")
    pool_count = pool_hidden.shape[0]
    per = hard_ids.shape[1] // owners
    column_count = batch_hidden.shape[0] * lax.axis_size("pa")
    members, size = lax.axis_size("pa"), batch_hidden.shape[0]
    pairs = members // 2
    term, weight = ((rows, depth), BF16), ((pool_count, rows), F32)

    ring = [0] + list(range(1, owners, 2)) + list(range(2, owners, 2))[::-1]

    def shift(x, k):
        to = [(ring[p], ring[(p + k) % owners]) for p in range(owners)]
        return lax.ppermute(x, "pb", to)

    def hold(x, others):
        return lax.optimization_barrier([x] + list(others))[0]

    def swap(x):
        return lax.ppermute(x, "pa", [(i, i ^ 1) for i in range(members)])

    def pass_on(x, step):
        return lax.ppermute(x, "pa", [(i, (i + 2 * step) % members) for i in range(members)])

    (packed,) = call(
        functools.partial(pack_kernel, owners, pool_count),
        [((rows + SUB, depth), BF16)],
        [],
        in_place=[
            pltpu.with_memory_space_constraint(hard_ids.T, pltpu.HBM),
            pltpu.with_memory_space_constraint(queries, pltpu.HBM),
        ],
        scratch=[
            pltpu.SemaphoreType.DMA,
            pltpu.VMEM(hard_ids.shape[::-1], jnp.int32),
            pltpu.SemaphoreType.DMA,
        ],
    )
    block = shift(packed, 1)
    other = swap(batch_hidden)
    table, turned, own_stat, own_weight, own_term = call(
        functools.partial(own_kernel, owners, per, scale),
        [((pool_count, depth), BF16), term, ((2, rows), F32), weight, term],
        [packed, pool_hidden, projection],
        flops=2 * depth * (pool_count * depth + rows * depth + 2 * rows * pool_count),
    )
    (chip,) = call(pair_kernel, [((2, size, depth), BF16)], [batch_hidden, other], flops=size * depth)
    chips = [chip] + [pass_on(chip, step) for step in range(1, pairs)]
    column, power, place, group_stat = call(
        functools.partial(group_kernel, scale, pairs),
        [
            ((column_count, depth), BF16),
            ((column_count, rows), F32),
            ((column_count, rows), F32),
            ((2, rows), F32),
        ],
        [queries, projection, query_group[None, :], group_lists] + chips,
        scratch=[pltpu.VMEM((pairs, 2, size, depth), BF16)],
        flops=2 * depth * column_count * (rows + depth),
    )
    stats, weights, terms, turned = [own_stat], [own_weight], [], [turned]
    direct = owners // 2 - 1
    waits, chain = [own_stat, chip], None
    for slot in range(1, owners):
        last = slot + 1 == owners
        later = None if last else shift(hold(block, waits), 1)
        one_stat, one_weight = call(
            functools.partial(score_kernel, owners, per, scale),
            [((2, rows), F32), weight],
            [table, block],
            after=turned[1:] if last else (),
            flops=2 * rows * pool_count * depth,
        )
        stats.append(one_stat)
        weights.append(one_weight)
        if last:
            (stat,) = call(
                join_kernel, [((2 * owners + 2, rows), F32)], stats + [group_stat], flops=rows
            )
        straight = slot <= direct or last
        shape = ((rows, depth), BF16) if straight else ((rows + SUB, depth), BF16)
        (one_term,) = call(
            term_kernel,
            [shape],
            [table, one_stat, one_weight] + ([] if chain is None else [chain]),
            flops=2 * rows * pool_count * depth,
        )
        if slot <= direct:
            terms.append((slot, one_term))
        else:
            chain = (slot, one_term)
            if not last:
                chain = shift(one_term, 1)
        turned += call(
            functools.partial(turn_kernel, 1),
            [term],
            [projection, block],
            after=[stat if last else one_stat],
            flops=2 * rows * depth * depth,
        )
        waits = [one_stat]
        block = later
    stats = [stat]
    for k in range(1, owners):
        stats.append(shift(stat, k))
    back = []
    for k, one in terms + [chain]:
        back.append(shift(hold(one, [stat]) if k <= direct else one, owners - k))
    terms = back
    keep, give, total, factor = call(
        functools.partial(soft_kernel, owners, direct, scale),
        [
            ((pairs, size, depth), F32),
            ((pairs * size, depth), BF16),
            ((rows, depth), F32),
            ((rows, rows), F32),
        ],
        [power, place, labels[None, :], turned[0], column, own_term] + stats,
        after=turned[-1:],
        flops=4 * rows * column_count * depth,
    )
    got = swap(give)
    parts = call(
        merge_kernel,
        [((size, depth), F32)] + [((size, depth), BF16)] * (pairs - 1),
        [keep, got.reshape(pairs, size, depth)],
        flops=column_count * depth,
    )
    for step in range(1, pairs):
        parts[step] = pass_on(parts[step], step)
    (pool_hidden_grad,) = call(
        functools.partial(pool_kernel, owners, scale),
        [((pool_count, depth), BF16)],
        stats + weights + turned,
        flops=2 * rows * owners * pool_count * depth,
    )
    query_grad, batch_hidden_grad = call(
        functools.partial(last_kernel, scale, len(parts)),
        [((rows, depth), BF16), (batch_hidden.shape, BF16)],
        [total, factor] + parts + terms,
        flops=4 * rows * depth * owners,
    )
    return (query_grad, batch_hidden_grad, pool_hidden_grad)


def solution(mesh):
    spread = P(("pa", "pb"))
    return jax.shard_map(
        shards,
        mesh=mesh,
        in_specs=(spread, spread, spread, P(), spread, spread, spread, P()),
        out_specs=(spread, spread, spread),
        check_vma=False,
    )
```

```python
import functools
import math

import jax
import jax.numpy as jnp
from jax import lax
from jax.experimental import pallas as pl
from jax.experimental.pallas import tpu as pltpu
from jax.sharding import PartitionSpec as P


F32 = jnp.float32
BF16 = jnp.bfloat16
LOW_BITS = 4
SUB = 8
VMEM_LIMIT = 8 << 20


def nn(a, b):
    return lax.dot_general(a, b, (((1,), (0,)), ((), ())), preferred_element_type=F32)


def nt(a, b):
    return lax.dot_general(a, b, (((1,), (1,)), ((), ())), preferred_element_type=F32)


def tn(a, b):
    return lax.dot_general(a, b, (((0,), (0,)), ((), ())), preferred_element_type=F32)


def tail_kernel(owners, pool_count, ids_hbm, tail_ref, ids_ref, ids_sem):
    hard_count, rows = ids_ref.shape
    per = hard_count // owners
    ids_copy = pltpu.make_async_copy(ids_hbm, ids_ref, ids_sem)
    ids_copy.start()
    tail_ref[...] = jnp.zeros(tail_ref.shape, BF16)
    ids_copy.wait()
    for block in range(hard_count // SUB):
        lines = []
        for place in range(block * SUB, (block + 1) * SUB):
            owner, j = divmod(place, per)
            k = j * owners + owner
            lines.append(ids_ref[k : k + 1, :] - owner * pool_count)
        ids = jnp.concatenate(lines, axis=0)
        high = jnp.right_shift(ids, LOW_BITS)
        low = ids - jnp.left_shift(high, LOW_BITS)
        start = 2 * block * rows
        tail_ref[:, start : start + rows] = high.astype(F32).astype(BF16)
        tail_ref[:, start + rows : start + 2 * rows] = low.astype(F32).astype(BF16)


def pack_kernel(query_ref, tail_ref, packed_ref):
    rows = query_ref.shape[0]
    packed_ref[:rows, :] = query_ref[...]
    packed_ref[rows:, :] = tail_ref[...]


def local_ids(tail_ref, me, rows, owners, per):
    base = tail_ref.shape[0] - SUB
    found = None
    for owner in range(owners):
        parts = []
        for j in range(per):
            block, sub = divmod(owner * per + j, SUB)
            start = 2 * block * rows
            high = tail_ref[base:, start : start + rows].astype(F32)
            low = tail_ref[base:, start + rows : start + 2 * rows].astype(F32)
            ids = high * float(1 << LOW_BITS) + low
            parts.append(ids[sub : sub + 1, :])
        if found is None:
            found = parts
        else:
            found = [jnp.where(me == owner, new, old) for new, old in zip(parts, found)]
    return found


def score_block(me, query_ref, tail_ref, table_ref, rows, owners, per, scale):
    count = table_ref.shape[0]
    ids = local_ids(tail_ref, me, rows, owners, per)
    dense = nt(table_ref[...], query_ref[:rows, :])
    row_iota = lax.broadcasted_iota(jnp.int32, (count, rows), 0).astype(F32)
    hits = [row_iota == one for one in ids]
    scores = [jnp.sum(jnp.where(hit, dense, 0.0), axis=0, keepdims=True) * scale for hit in hits]
    top = functools.reduce(jnp.maximum, scores)
    powers = [jnp.exp(one - top) for one in scores]
    weight = jnp.zeros((count, rows), F32)
    for hit, one in zip(hits, powers):
        weight = weight + jnp.where(hit, one, 0.0)
    return weight, top, functools.reduce(jnp.add, powers)


def table_kernel(hidden_ref, projection_ref, table_ref):
    table_ref[...] = nn(hidden_ref[...], projection_ref[...]).astype(BF16)


def own_kernel(owners, per, scale, query_ref, tail_ref, table_ref, projection_ref, *outs):
    turned_ref, stat_ref, weight_ref, term_ref = outs
    me = lax.axis_index("pb")
    rows = query_ref.shape[0]
    turned_ref[...] = nt(query_ref[...], projection_ref[...]).astype(BF16)
    weight, top, total = score_block(
        me, query_ref, tail_ref, table_ref, rows, owners, per, scale
    )
    stat_ref[0:1, :] = top
    stat_ref[1:2, :] = total
    weight_ref[...] = weight
    term_ref[...] = tn(weight.astype(BF16), table_ref[...]).astype(BF16)


def score_kernel(owners, per, scale, table_ref, packed_ref, stat_ref, weight_ref):
    rows = packed_ref.shape[0] - SUB
    me = lax.axis_index("pb")
    weight, top, total = score_block(me, packed_ref, packed_ref, table_ref, rows, owners, per, scale)
    stat_ref[0:1, :] = top
    stat_ref[1:2, :] = total
    weight_ref[...] = weight


def term_kernel(table_ref, stat_ref, weight_ref, *refs):
    old_ref, out_ref = refs if len(refs) == 2 else (None, refs[0])
    weight, top = weight_ref[...], stat_ref[0:1, :]
    rows = weight.shape[1]
    if old_ref is not None:
        parts = [old_ref[rows:, k * rows : (k + 1) * rows].astype(F32)[0:1, :] for k in range(3)]
        before = parts[0] + parts[1] + parts[2]
        both = jnp.maximum(before, top)
        weight = weight * jnp.exp(top - both)
        column = jnp.broadcast_to(jnp.exp(before - both), (rows, rows)).T[:, :1]
        top = both
    term = tn(weight.astype(BF16), table_ref[...])
    if old_ref is not None:
        term = term + column * old_ref[:rows, :].astype(F32)
    out_ref[:rows, :] = term.astype(BF16)
    if out_ref.shape[0] > rows:
        out_ref[rows:, :] = jnp.zeros((SUB, out_ref.shape[1]), BF16)
        left = jnp.broadcast_to(top, (SUB, rows))
        for k in range(3):
            part = left.astype(BF16)
            out_ref[rows:, k * rows : (k + 1) * rows] = part
            left = left - part.astype(F32)


def join_kernel(*refs):
    for k, ref in enumerate(refs[:-1]):
        refs[-1][2 * k : 2 * k + 2, :] = ref[...]


def pair_kernel(mine_ref, other_ref, out_ref):
    first = lax.rem(lax.axis_index("pa"), 2) == 0
    mine, other = mine_ref[...], other_ref[...]
    out_ref[0] = jnp.where(first, mine, other)
    out_ref[1] = jnp.where(first, other, mine)


def turn_kernel(count, projection_ref, *refs):
    for packed_ref, out_ref in zip(refs[:count], refs[-count:]):
        rows = out_ref.shape[0]
        out_ref[...] = nt(packed_ref[:rows, :], projection_ref[...]).astype(BF16)


def group_kernel(scale, pairs, query_ref, projection_ref, group_ref, lists_ref, *refs):
    column_ref, power_ref, place_ref, stat_ref, hidden_ref = refs[pairs:]
    rows = query_ref.shape[0]
    groups, size = lists_ref.shape
    count = column_ref.shape[0]
    pair = lax.div(lax.axis_index("pa"), 2)
    for step, ref in enumerate(refs[:pairs]):
        hidden_ref[lax.rem(pair - step + pairs, pairs)] = ref[...]
    hidden = hidden_ref[...].reshape(count, query_ref.shape[1])
    column_ref[...] = nn(hidden, projection_ref[...]).astype(BF16)
    dense = nt(column_ref[...], query_ref[...]) * scale
    column_iota = lax.broadcasted_iota(jnp.int32, (groups, count), 1)
    places = jnp.zeros((groups, count), F32)
    lists = lists_ref[...]
    for c in range(size):
        places = places + jnp.where(lists[:, c : c + 1] == column_iota, float(c + 1), 0.0)
    group_iota = lax.broadcasted_iota(jnp.int32, (groups, rows), 0)
    mine = (group_iota == group_ref[...]).astype(F32).astype(BF16)
    place = tn(places.astype(BF16), mine)
    member = place > 0.5
    top = jnp.max(jnp.where(member, dense, -jnp.inf), axis=0, keepdims=True)
    power = jnp.where(member, jnp.exp(jnp.where(member, dense - top, 0.0)), 0.0)
    power_ref[...] = power
    place_ref[...] = place
    stat_ref[0:1, :] = top
    stat_ref[1:2, :] = jnp.sum(power, axis=0, keepdims=True)


def totals(stat_refs, owners, source):
    group_ref = stat_refs[source]
    tops = [group_ref[2 * owners : 2 * owners + 1, :]]
    sums = [group_ref[2 * owners + 1 : 2 * owners + 2, :]]
    for step, ref in enumerate(stat_refs):
        slot = (source - step) % owners
        tops.append(ref[2 * slot : 2 * slot + 1, :])
        sums.append(ref[2 * slot + 1 : 2 * slot + 2, :])
    top = functools.reduce(jnp.maximum, tops)
    total = functools.reduce(jnp.add, [s * jnp.exp(t - top) for s, t in zip(sums, tops)])
    return top, total


def soft_kernel(owners, direct, scale, *refs):
    power_ref, place_ref, label_ref, turned_ref, column_ref, own_term_ref = refs[:6]
    stat_refs = refs[6 : 6 + owners]
    keep_ref, give_ref, sum_ref, factor_ref = refs[6 + owners :]
    rows = turned_ref.shape[0]
    top, total = totals(stat_refs, owners, 0)
    place = place_ref[...]
    target = (place == (label_ref[...] + 1).astype(F32)).astype(F32)
    group_top = stat_refs[0][2 * owners : 2 * owners + 1, :]
    likely = power_ref[...] * jnp.exp(group_top - top) / total
    grad = jnp.where(place > 0.5, likely - target, 0.0)
    kept, _, size, _ = halves = (keep_ref.shape[0], 2, keep_ref.shape[1], rows)
    even, odd = grad.reshape(halves)[:, 0], grad.reshape(halves)[:, 1]
    first = lax.rem(lax.axis_index("pa"), 2) == 0
    mine = jnp.where(first, even, odd).reshape(kept * size, rows).astype(BF16)
    other = jnp.where(first, odd, even).reshape(kept * size, rows).astype(BF16)
    give_ref[...] = (nn(other, turned_ref[...]) * scale).astype(BF16)
    keep_ref[...] = (nn(mine, turned_ref[...]) * scale).reshape(keep_ref.shape)
    tops = [stat_refs[(owners - k) % owners][2 * k : 2 * k + 1, :] for k in range(owners)]
    tops = tops[: direct + 1] + [functools.reduce(jnp.maximum, tops[direct + 1 :])]
    factor = [jnp.exp(one - top) / total for one in tops]
    factor = jnp.concatenate(factor + [jnp.zeros((rows - direct - 2, rows), F32)], axis=0).T
    factor_ref[...] = factor
    own = factor[:, :1] * own_term_ref[...].astype(F32)
    sum_ref[...] = tn(grad.astype(BF16), column_ref[...]) + own


def merge_kernel(keep_ref, got_ref, own_ref, *outs):
    pairs = keep_ref.shape[0]
    pair = lax.div(lax.axis_index("pa"), 2)
    own_ref[...] = keep_ref[pair] + got_ref[pair].astype(F32)
    for step in range(1, pairs):
        to = lax.rem(pair + step, pairs)
        outs[step - 1][...] = (keep_ref[to] + got_ref[to].astype(F32)).astype(BF16)


def pool_kernel(owners, scale, *refs):
    stat_refs = refs[:owners]
    weight_refs = refs[owners : 2 * owners]
    turned_refs = refs[2 * owners : 3 * owners]
    out_ref = refs[3 * owners]
    acc = None
    for source in range(owners):
        top, total = totals(stat_refs, owners, source)
        factor = jnp.exp(stat_refs[0][2 * source : 2 * source + 1, :] - top) / total
        part = nn((weight_refs[source][...] * factor).astype(BF16), turned_refs[source][...])
        acc = part if acc is None else acc + part
    out_ref[...] = (acc * scale).astype(BF16)


def last_kernel(scale, parts, sum_ref, factor_ref, *refs):
    query_ref, batch_ref = refs[-2:]
    batch_ref[...] = functools.reduce(
        jnp.add, [ref[...].astype(F32) for ref in refs[:parts]]
    ).astype(BF16)
    total = sum_ref[...]
    for k, ref in enumerate(refs[parts:-2]):
        total = total + factor_ref[:, k + 1 : k + 2] * ref[...].astype(F32)
    query_ref[...] = (total * scale).astype(BF16)


def call(kernel, outs, arrays, after=(), flops=0, in_place=(), scratch=()):
    outs = [jax.ShapeDtypeStruct(*one) for one in outs]
    arrays = list(arrays) + list(in_place)
    moved = sum(a.size * a.dtype.itemsize for a in arrays + outs)
    count, waits = len(arrays), len(after)
    vmem = pl.BlockSpec(memory_space=pltpu.VMEM)

    def body(*refs):
        kernel(*refs[:count], *refs[count + waits :])

    results = pl.pallas_call(
        body,
        out_shape=outs,
        in_specs=[vmem] * (len(arrays) - len(in_place))
        + [pl.BlockSpec(memory_space=pltpu.HBM)] * len(in_place)
        + [pl.BlockSpec(memory_space=pl.ANY)] * waits,
        out_specs=[vmem] * len(outs),
        scratch_shapes=list(scratch),
        compiler_params=pltpu.CompilerParams(vmem_limit_bytes=VMEM_LIMIT),
        cost_estimate=pl.CostEstimate(flops=flops, bytes_accessed=moved, transcendentals=0),
    )(*arrays, *after)
    return list(results)


def shards(
    queries, batch_hidden, pool_hidden, projection, hard_ids, query_group, labels, group_lists
):
    rows, depth = queries.shape
    scale = 1.0 / math.sqrt(depth)
    owners = lax.axis_size("pb")
    pool_count = pool_hidden.shape[0]
    per = hard_ids.shape[1] // owners
    column_count = batch_hidden.shape[0] * lax.axis_size("pa")
    members, size = lax.axis_size("pa"), batch_hidden.shape[0]
    pairs = members // 2
    term, weight = ((rows, depth), BF16), ((pool_count, rows), F32)

    ring = [0] + list(range(1, owners, 2)) + list(range(2, owners, 2))[::-1]

    def shift(x, k):
        to = [(ring[p], ring[(p + k) % owners]) for p in range(owners)]
        return lax.ppermute(x, "pb", to)

    def hold(x, others):
        return lax.optimization_barrier([x] + list(others))[0]

    def swap(x):
        return lax.ppermute(x, "pa", [(i, i ^ 1) for i in range(members)])

    def pass_on(x, step):
        return lax.ppermute(x, "pa", [(i, (i + 2 * step) % members) for i in range(members)])

    first = shift(queries, 1)
    (tail,) = call(
        functools.partial(tail_kernel, owners, pool_count),
        [((SUB, depth), BF16)],
        [],
        in_place=[pltpu.with_memory_space_constraint(hard_ids.T, pltpu.HBM)],
        scratch=[pltpu.VMEM(hard_ids.shape[::-1], jnp.int32), pltpu.SemaphoreType.DMA],
    )
    first_tail = shift(tail, 1)
    (block,) = call(
        pack_kernel, [((rows + SUB, depth), BF16)], [first, first_tail], flops=rows * depth
    )
    other = swap(batch_hidden)
    (table,) = call(
        table_kernel,
        [((pool_count, depth), BF16)],
        [pool_hidden, projection],
        flops=2 * depth * pool_count * depth,
    )
    turned, own_stat, own_weight, own_term = call(
        functools.partial(own_kernel, owners, per, scale),
        [term, ((2, rows), F32), weight, term],
        [queries, tail, table, projection],
        flops=2 * depth * (rows * depth + 2 * rows * pool_count),
    )
    (chip,) = call(pair_kernel, [((2, size, depth), BF16)], [batch_hidden, other], flops=size * depth)
    chips = [chip] + [pass_on(chip, step) for step in range(1, pairs)]
    column, power, place, group_stat = call(
        functools.partial(group_kernel, scale, pairs),
        [
            ((column_count, depth), BF16),
            ((column_count, rows), F32),
            ((column_count, rows), F32),
            ((2, rows), F32),
        ],
        [queries, projection, query_group[None, :], group_lists] + chips,
        scratch=[pltpu.VMEM((pairs, 2, size, depth), BF16)],
        flops=2 * depth * column_count * (rows + depth),
    )
    stats, weights, terms, turned = [own_stat], [own_weight], [], [turned]
    direct = owners // 2 - 1
    waits, chain = [chip, table], None
    for slot in range(1, owners):
        last = slot + 1 == owners
        later = None if last else shift(hold(block, waits), 1)
        one_stat, one_weight = call(
            functools.partial(score_kernel, owners, per, scale),
            [((2, rows), F32), weight],
            [table, block],
            after=turned[1:] if last else (),
            flops=2 * rows * pool_count * depth,
        )
        stats.append(one_stat)
        weights.append(one_weight)
        if last:
            (stat,) = call(
                join_kernel, [((2 * owners + 2, rows), F32)], stats + [group_stat], flops=rows
            )
        straight = slot <= direct or last
        shape = ((rows, depth), BF16) if straight else ((rows + SUB, depth), BF16)
        (one_term,) = call(
            term_kernel,
            [shape],
            [table, one_stat, one_weight] + ([] if chain is None else [chain]),
            flops=2 * rows * pool_count * depth,
        )
        if slot <= direct:
            terms.append((slot, one_term))
        else:
            chain = (slot, one_term)
            if not last:
                chain = shift(one_term, 1)
        turned += call(
            functools.partial(turn_kernel, 1),
            [term],
            [projection, block],
            after=[stat if last else one_stat],
            flops=2 * rows * depth * depth,
        )
        waits = [one_stat]
        block = later
    stats = [stat]
    for k in range(1, owners):
        stats.append(shift(stat, k))
    back = []
    for k, one in terms + [chain]:
        back.append(shift(hold(one, [stat]) if k <= direct else one, owners - k))
    terms = back
    keep, give, total, factor = call(
        functools.partial(soft_kernel, owners, direct, scale),
        [
            ((pairs, size, depth), F32),
            ((pairs * size, depth), BF16),
            ((rows, depth), F32),
            ((rows, rows), F32),
        ],
        [power, place, labels[None, :], turned[0], column, own_term] + stats,
        after=turned[-1:],
        flops=4 * rows * column_count * depth,
    )
    got = swap(give)
    parts = call(
        merge_kernel,
        [((size, depth), F32)] + [((size, depth), BF16)] * (pairs - 1),
        [keep, got.reshape(pairs, size, depth)],
        flops=column_count * depth,
    )
    for step in range(1, pairs):
        parts[step] = pass_on(parts[step], step)
    (pool_hidden_grad,) = call(
        functools.partial(pool_kernel, owners, scale),
        [((pool_count, depth), BF16)],
        stats + weights + turned,
        flops=2 * rows * owners * pool_count * depth,
    )
    query_grad, batch_hidden_grad = call(
        functools.partial(last_kernel, scale, len(parts)),
        [((rows, depth), BF16), (batch_hidden.shape, BF16)],
        [total, factor] + parts + terms,
        flops=4 * rows * depth * owners,
    )
    return (query_grad, batch_hidden_grad, pool_hidden_grad)


def solution(mesh):
    spread = P(("pa", "pb"))
    return jax.shard_map(
        shards,
        mesh=mesh,
        in_specs=(spread, spread, spread, P(), spread, spread, spread, P()),
        out_specs=(spread, spread, spread),
        check_vma=False,
    )
```
